32 devices in a mesh: groups: 2 (over x), expert: 16 (over z, y, core).
Axes of the slice: x: 2, y: 2, z: 4, core: 2. Of those that a mesh axis runs over, the one named last changes fastest.
Arguments:
- tokens: bfloat16 [2, 2048, 2048], P(None, ('groups', 'expert')), parts along dimension 1, may hold values from -6 to 6
- w_gate: bfloat16 [16, 2048, 768], P('expert'), may hold values from -0.125 to 0.125
- w_up: bfloat16 [16, 2048, 768], P('expert'), may hold values from -0.125 to 0.125
- w_down: bfloat16 [16, 768, 2048], P('expert'), may hold values from -0.21875 to 0.21875
- hot_gate: bfloat16 [2, 2048, 768], P(None, None, 'expert'), may hold values from -0.125 to 0.125
- hot_up: bfloat16 [2, 2048, 768], P(None, None, 'expert'), may hold values from -0.125 to 0.125
- hot_down: bfloat16 [2, 2048, 768], P(None, None, 'expert'), may hold values from -0.21875 to 0.21875
- cold_routes: int32 [2, 2048, 7], P(None, ('groups', 'expert')), parts along dimension 1, may hold values from 0 to 15, all different within a row; in each aligned block of 64 rows (0 to 63, 64 to 127, ..., all dimensions but the last counted through in order) at most 43 rows name the same one
- hot_pick: int32 [2, 2048], P(None, ('groups', 'expert')), parts along dimension 1, may hold values from 0 to 1, as said below
- gates: float32 [2, 2048, 8], P(None, ('groups', 'expert')), parts along dimension 1, may hold values from 0.1 to 1
Outputs:
- mixed: bfloat16 [2, 2048, 2048], P(None, ('groups', 'expert')), parts along dimension 1
The draws below stay inside these ranges and needn't reach their ends.
There are 2 independent parts, one for each index of `groups`. The reference program is written for one: setup_inputs(seed, part) draws one part's arguments, and reference() takes and returns one part's arrays. A program takes and returns all parts, laid end to end along the dimension named above; an argument that names none is the same for every part. Nothing has to cross between parts.
Inputs may be any that keep to these rules, and one draw needn't show every extreme that they name: `hot_pick`: in each aligned block of 64 tokens of one micro-batch, each hot expert is picked by exactly 32 tokens. `cold_routes`: A token names 8 - 1 different cold experts; in each aligned block of 64 tokens of one micro-batch no cold expert is named more than 43 times.
All inputs are finite; a program needn't handle non-finite values.
Results may differ from the reference program's by a relative error of at most 0.0058.
Values may be sent and summed in bfloat16 or wider, within the bound.
A program may use at most 128 MiB of HBM per device.

```python
import math
import jax
import jax.numpy as jnp
import numpy as np
from jax import lax

D = 2048
FF = 768
TOP = 8
HOT = 2
MB = 2
TOK_DEV = 64
COLD = 16
TOKENS = 1024
CAP = 43
N_EXPERT = 16


def draw_hot_pick(key, part):
    blocks = MB * TOKENS // TOK_DEV
    keys = jax.random.split(key, blocks)

    def one_block(block_key):
        return jax.random.permutation(block_key, TOK_DEV)
    orders = jax.vmap(one_block)(keys)
    return (orders % HOT).astype(jnp.int32).reshape(MB, TOKENS)


def block_scale(own_key, extent, cuts, smallest, top_value):
    def one(position, shards_of):
        heights = jax.random.uniform(jax.random.fold_in(jax.random.fold_in(own_key, 6), position), (shards_of,), jnp.float32, smallest / len(cuts), top_value / len(cuts))
        return jnp.repeat(jnp.exp(heights), extent[position] // shards_of).reshape((-1,) + (1,) * (len(extent) - position - 1))

    level = one(*cuts[0])
    for cut in cuts[1:]:
        level = level * one(*cut)
    return level


def deal_out(own_key, own, number, rows, amount, top, most, slope):
    sequence = jax.random.permutation(own_key, amount)
    packed, common = shares(amount, rows * top, most, slope, True), shares(amount, rows * top, most, slope, False)
    places = jnp.arange(amount)

    def named(sizes, offset_by):
        used = int((sizes > 0).sum())
        fixed = max(1, used // 4)
        moved = fixed + (places - fixed + offset_by * (used - fixed)) % max(1, amount - fixed)
        return jnp.zeros((amount,), jnp.int32).at[sequence[jnp.where(places < fixed, places, moved)]].set(jnp.asarray(sizes, jnp.int32))

    sizes = jnp.where(number % 4 == 0, named(packed, number // 4), named(common, number - number // 4 - 1))
    mixed = jax.random.permutation(jax.random.fold_in(own, 3), amount)
    source_of, taker = mixed[0:amount // 2 * 2:2], mixed[1:amount // 2 * 2:2]
    room = jnp.minimum(sizes[source_of] - 1, most - sizes[taker]) // 2
    room = jnp.where((source_of == sequence[0]) | (taker == sequence[0]) | (sizes[taker] == 0), 0, jnp.maximum(room, 0))
    moved = jax.random.randint(jax.random.fold_in(own, 4), (amount // 2,), 0, 1 << 20) % (room + 1)
    sizes = sizes.at[source_of].add(-moved).at[taker].add(moved)
    labels = jnp.searchsorted(jnp.cumsum(sizes), jnp.arange(rows * top), side="right").astype(jnp.int32)
    table = labels.reshape(top, rows).T
    table = table[jax.random.permutation(jax.random.fold_in(own, 1), rows)]
    offset_by = jax.random.randint(jax.random.fold_in(own, 2), (rows, 1), 0, top)
    return jnp.take_along_axis(table, (jnp.arange(top)[None, :] + offset_by) % top, axis=1)


def shares(number_of, total, reach, slope, full):
    loads = [(1 << 20) // math.isqrt(rank ** slope) + 1 for rank in range(1, number_of + 1)]
    largest = reach if full else min(reach, max(-(-total // number_of), total * loads[0] // sum(loads)))
    least = 1 if total - largest >= number_of - 1 else 0
    holding, spare = [largest] + [least] * (number_of - 1), total - largest - least * (number_of - 1)
    while spare > 0:
        candidates = [i for i in range(1, number_of) if holding[i] < largest] or [i for i in range(1, number_of) if holding[i] < reach]
        mass, budget = sum([loads[i] for i in candidates]), spare
        for i in candidates:
            more = min(reach - holding[i], max(1, budget * loads[i] // mass), spare)
            holding[i] = holding[i] + more
            spare = spare - more
    return np.array(holding)


def noise(stream_key, shape, width, most, cuts=(), kind=jnp.bfloat16):
    loudness = block_scale(stream_key, shape, cuts, -0.22, 0.18) if cuts else 1.0
    array = jax.random.normal(stream_key, shape, jnp.float32) * width * loudness
    return jnp.minimum(jnp.maximum(array, -most), most).astype(kind)


def setup_inputs(seed: int = 0, part: int = 0) -> dict:
    seeds = jax.random.split(jax.random.key(seed), 11)
    part_splits = jax.random.split(jax.random.fold_in(seeds[10], part), 11)
    tokens = noise(part_splits[0], (MB, TOKENS, D), 1.0, 6.0, ((1, 16),))
    w_gate = noise(seeds[1], (COLD, D, FF), D ** -0.5, 0.125, ((0, 16),))
    w_up = noise(seeds[2], (COLD, D, FF), D ** -0.5, 0.125, ((0, 16),))
    w_down = noise(seeds[3], (COLD, FF, D), FF ** -0.5, 0.21875, ((0, 16),))
    hot_gate = noise(seeds[4], (HOT, D, FF), D ** -0.5, 0.125, ((2, 16),))
    hot_up = noise(seeds[5], (HOT, D, FF), D ** -0.5, 0.125, ((2, 16),))
    hot_down = noise(seeds[6], (HOT, D, FF), FF ** -0.5, 0.21875, ((2, 16),))
    cold_routes_keys = jax.random.split(jax.random.fold_in(part_splits[7], 1), MB * TOKENS // TOK_DEV)
    cold_routes_turns = jax.random.permutation(jax.random.fold_in(part_splits[7], 3), MB * TOKENS // TOK_DEV)
    cold_routes = jax.vmap(lambda own, number: deal_out(jax.random.fold_in(part_splits[7], 2), own, number, TOK_DEV, COLD, TOP - 1, CAP, 2))(cold_routes_keys, cold_routes_turns).reshape((MB, TOKENS, TOP - 1))
    hot_pick = draw_hot_pick(jax.random.fold_in(jax.random.fold_in(seeds[10], part), 71), part)
    gates = jnp.clip(jnp.exp(math.log(1.0) - 2.3025851 * jax.random.uniform(part_splits[9], (MB, TOKENS, TOP), jnp.float32) ** block_scale(part_splits[9], (MB, TOKENS, TOP), ((1, 16),), -0.2, 0.2)), 0.1, 1.0)
    return {"tokens": tokens, "w_gate": w_gate, "w_up": w_up, "w_down": w_down, "hot_gate": hot_gate, "hot_up": hot_up, "hot_down": hot_down, "cold_routes": cold_routes, "hot_pick": hot_pick, "gates": gates}


def expert_rows(rows_in, gate_one, up_one, down_one):
    gate = jnp.dot(rows_in, gate_one, preferred_element_type=jnp.float32)
    upward = jnp.dot(rows_in, up_one, preferred_element_type=jnp.float32)
    hidden = (jax.nn.silu(gate) * upward).astype(jnp.bfloat16)
    return jnp.dot(hidden, down_one, preferred_element_type=jnp.float32).astype(jnp.bfloat16)


def reference(tokens, w_gate, w_up, w_down, hot_gate, hot_up, hot_down, cold_routes, hot_pick, gates):
    all_rows = MB * TOKENS
    picks = TOP - 1
    flat = tokens.reshape(all_rows, D)
    expert = cold_routes.reshape(all_rows * picks)
    owner = jnp.repeat(jnp.arange(all_rows, dtype=jnp.int32), picks)
    weight = gates[:, :, 1:].reshape(all_rows * picks)
    bound = MB * N_EXPERT * CAP

    def visit(carry, number):
        chosen = expert == number
        found = jnp.nonzero(chosen, size=bound, fill_value=0)[0].astype(jnp.int32)
        live = jnp.arange(bound, dtype=jnp.int32) < jnp.sum(chosen.astype(jnp.int32))
        rows_at = owner[found]
        result = expert_rows(flat[rows_at], w_gate[number], w_up[number], w_down[number])
        scaled = jnp.where(live, weight[found], jnp.zeros_like(weight[found]))[:, None] * result.astype(jnp.float32)
        return carry.at[rows_at].add(scaled), None

    total = jnp.zeros((all_rows, D), jnp.float32)
    total, unused = lax.scan(visit, total, jnp.arange(COLD, dtype=jnp.int32))
    pick_flat = hot_pick.reshape(all_rows)
    share = all_rows // HOT
    hot_gate_row = gates[:, :, 0].reshape(all_rows)
    for number in range(HOT):
        found = jnp.nonzero(pick_flat == number, size=share, fill_value=0)[0].astype(jnp.int32)
        result = expert_rows(flat[found], hot_gate[number], hot_up[number], jnp.transpose(hot_down[number]))
        total = total.at[found].add(hot_gate_row[found][:, None] * result.astype(jnp.float32))
    return total.astype(jnp.bfloat16).reshape(MB, TOKENS, D)
```

```python
import functools

import jax
import jax.numpy as jnp
from jax import lax
from jax.experimental import pallas as pl
from jax.experimental.pallas import tpu as pltpu
from jax.sharding import PartitionSpec as P

TOP = 8
HOT = 2


def expert_rows(rows_in, weights):
    leading = rows_in.shape[:-1]
    flat_rows = rows_in.reshape(-1, rows_in.shape[-1])
    gate = jnp.dot(flat_rows, weights[0], preferred_element_type=jnp.float32)
    upward = jnp.dot(flat_rows, weights[1], preferred_element_type=jnp.float32)
    hidden = (jax.nn.silu(gate) * upward).astype(jnp.bfloat16)
    result = jnp.dot(hidden, weights[2], preferred_element_type=jnp.float32).astype(jnp.bfloat16)
    return result.reshape(leading + (result.shape[-1],))


def slot_table(routes_block, axis_width, capacity):
    expert = routes_block.reshape(-1)
    total_count = expert.shape[0]
    onehot = (expert[:, None] == jnp.arange(axis_width, dtype=jnp.int32)[None, :]).astype(jnp.int32)
    before = jnp.cumsum(onehot, axis=0) - onehot
    slot_rank = jnp.sum(before * onehot, axis=1)
    slot_place = expert * capacity + slot_rank
    target = jnp.arange(axis_width * capacity, dtype=jnp.int32)
    matched = slot_place[None, :] == target[:, None]
    filled = jnp.any(matched, axis=1)
    source = jnp.sum(
        jnp.where(matched, jnp.arange(total_count, dtype=jnp.int32)[None, :], 0), axis=1
    )
    return (slot_place, source, filled)


def routed(tokens, w_gate, w_up, w_down, hot_gate, hot_up, hot_down, cold_routes, hot_pick, gates):
    axis_width = lax.axis_size("expert")
    micro_count, local_tokens, model_width = tokens.shape
    picks = TOP - 1
    capacity = local_tokens * picks * 3 // (2 * axis_width) + 1
    own_weights = (w_gate[0], w_up[0], w_down[0])
    outbound = []
    tables = []
    for micro in range(micro_count):
        slot_place, source, filled = slot_table(cold_routes[micro], axis_width, capacity)
        rows_out = tokens[micro][source // picks]
        rows_out = jnp.where(filled[:, None], rows_out, jnp.zeros_like(rows_out))
        outbound.append(rows_out.reshape(axis_width, capacity, model_width))
        tables.append(slot_place)
    joined = jnp.concatenate(outbound, axis=1)
    back_all = lax.all_to_all(
        expert_rows(
            lax.all_to_all(joined, "expert", split_axis=0, concat_axis=0, tiled=True), own_weights
        ),
        "expert",
        split_axis=0,
        concat_axis=0,
        tiled=True,
    )
    returned = [
        back_all[:, micro * capacity : (micro + 1) * capacity] for micro in range(micro_count)
    ]
    cold_parts = []
    for micro in range(micro_count):
        picked = returned[micro].reshape(axis_width * capacity, model_width)[tables[micro]]
        picked = picked.reshape(local_tokens, picks, model_width).astype(jnp.float32)
        cold_parts.append(jnp.sum(picked * gates[micro, :, 1:, None], axis=1))
    cold_total = jnp.stack(cold_parts)
    all_rows = micro_count * local_tokens
    flat = tokens.reshape(all_rows, model_width)
    order = jnp.argsort(hot_pick.reshape(all_rows), stable=True)
    share = all_rows // HOT
    grouped = flat[order].reshape(HOT, share, model_width)
    gate = jnp.einsum(
        "hsd,hdf->hsf",
        grouped,
        lax.all_gather(hot_gate, "expert", axis=2, tiled=True),
        preferred_element_type=jnp.float32,
    )
    upward = jnp.einsum(
        "hsd,hdf->hsf",
        grouped,
        lax.all_gather(hot_up, "expert", axis=2, tiled=True),
        preferred_element_type=jnp.float32,
    )
    hidden = (jax.nn.silu(gate) * upward).astype(jnp.bfloat16)
    hot_sum = jnp.einsum(
        "hsf,hdf->hsd",
        hidden,
        lax.all_gather(hot_down, "expert", axis=2, tiled=True),
        preferred_element_type=jnp.float32,
    )
    sorted_out = hot_sum.astype(jnp.bfloat16).reshape(all_rows, model_width)
    inverse = jnp.argsort(order)
    hot_out = sorted_out[inverse].astype(jnp.float32) * gates[:, :, 0].reshape(all_rows)[:, None]
    total = hot_out.reshape(micro_count, local_tokens, model_width) + cold_total
    return total.astype(jnp.bfloat16)


CHUNKS = 4
GATHER_FAR = 3
REDUCE_NEAR = 2
ROOM = 56 * 2**20


def column(row):
    rows = row.shape[1]
    down = lax.broadcasted_iota(jnp.int32, (rows, rows), 0)
    across = lax.broadcasted_iota(jnp.int32, (rows, rows), 1)
    return jnp.sum(jnp.where(down == across, row, 0.0), axis=1, keepdims=True)


def tile_of(extent, most):
    return most if extent % most == 0 else extent


def fused(
    n, hot, part, tok, routes, pick, gts, wg_in, wu_in, wd_in, hg_in, hu_in, hd_in, out,
    xs, keep, sc, rc, sy, ry, sz, rz, wg, wu, wd, wh, hid, hhid, cs, ct,
    wsem, tsem, cts, ctr, up_s, down_s, z_r, y_s, y_r, c_s, c_r,
    rc_s, rc_r, ry_s, ry_r, rz_s, rz_r,
):
    nz = n // 4
    rows, model = tok.shape
    units = wg.shape[1]
    pad = hhid.shape[1]
    piece = rows // CHUNKS
    wide = tile_of(units, 256)
    tile = tile_of(model, 512)
    tiles = model // tile
    me = lax.axis_index("expert")
    c = lax.rem(me, 2)
    y = lax.rem(lax.div(me, 2), 2)
    z = lax.div(me, 4)
    own = y * 2 + c
    side = (1 - y) * 2 + c
    peer_y = z * 4 + side
    peer_c = z * 4 + y * 2 + (1 - c)
    corner = (z == 0) | (z == nz - 1)

    def remote(src, dst, send, recv, device):
        return pltpu.make_async_remote_copy(
            src_ref=src, dst_ref=dst, send_sem=send, recv_sem=recv,
            device_id={"expert": device}, device_id_type=pl.DeviceIdType.MESH,
        )

    def span(k):
        return pl.ds(pl.multiple_of(k * piece, piece), piece)

    loads = [
        pltpu.make_async_copy(src, dst, wsem.at[i])
        for i, (src, dst) in enumerate((
            *(
                (src.at[h], wh.at[pl.ds(t * pad + h * part, part)])
                for t, src in enumerate((hg_in, hu_in, hd_in)) for h in range(hot)
            ),
            (wg_in, wg), (wu_in, wu), (wd_in, wd),
        ))
    ]
    first = pltpu.make_async_copy(tok, xs.at[z, own], tsem)
    first.start()
    for load in loads:
        load.start()

    barrier = pltpu.get_barrier_semaphore()

    @pl.loop(1, n)
    def _(i):
        pl.semaphore_signal(
            barrier, inc=1, device_id={"expert": lax.rem(me + i, n)},
            device_id_type=pl.DeviceIdType.MESH,
        )

    if pad > hot * part:
        for t in range(3):
            blank = wh.at[pl.ds(t * pad + hot * part, pad - hot * part)]
            blank[...] = jnp.zeros_like(blank)

    ct[...] = jnp.zeros_like(ct)
    micros = gts.shape[0]

    def joined(parts):
        return jnp.concatenate(parts, axis=1)

    warm_row = joined([gts[m, 0:1, :] for m in range(micros)])
    chosen = joined([pick[m : m + 1, :] for m in range(micros)])
    named = [
        (
            joined([routes[k, m : m + 1, :] for m in range(micros)]),
            joined([gts[m, k + 1 : k + 2, :] for m in range(micros)]),
        )
        for k in range(routes.shape[0])
    ]

    def row(e):
        return sum(jnp.where(route == e, weight, 0.0) for route, weight in named)

    for e in range(n):
        ct[e, 0:1, :] = row(e)
        for h in range(hot):
            ct[e, 1 + h : 2 + h, :] = jnp.where(chosen == h, warm_row, 0.0)

    cs[me] = ct[me]
    pl.semaphore_wait(barrier, n - 1)

    def ct_copy(i):
        peer = lax.rem(me + i, n)
        return remote(ct.at[peer], cs.at[me], cts.at[i], ctr.at[me], peer)

    def go_own(p, k, send, device):
        ref = xs.at[p, own, span(k)]
        return remote(ref, ref, send.at[p, k], z_r.at[p, k], device)

    def go_side(p, k, send, device):
        ref = xs.at[p, side, span(k)]
        at = CHUNKS + k - GATHER_FAR
        return remote(ref, ref, send.at[p, at], z_r.at[p, at], device)

    def go_y(p, k):
        ref = xs.at[p, own, span(k)]
        return remote(ref, ref, y_s.at[p, k], y_r.at[p, k], peer_y)

    def go_c(p, which):
        ref = xs.at[p, own if which == 0 else side]
        return remote(ref, ref, c_s.at[p, which], c_r.at[p, which], peer_c)

    def relay(p, k, go):
        @pl.when((p <= z) & (z + 1 < nz))
        def _():
            go(p, k, up_s, me + 4).start()

        @pl.when((p >= z) & (z > 0))
        def _():
            go(p, k, down_s, me - 4).start()

    def at_distance(d, act):
        @pl.when(z - d >= 0)
        def _():
            act(z - d)

        @pl.when(z + d < nz)
        def _():
            act(z + d)

    def serve_own(d, k):
        def act(p):
            go_own(p, k, up_s, me).wait_recv()
            relay(p, k, go_own)

            @pl.when(k < GATHER_FAR)
            def _():
                go_y(p, k).start()

            @pl.when(k == CHUNKS - 1)
            def _():
                go_c(p, 0).start()

        at_distance(d, act)

    def serve_side(d):
        def act(p):
            @pl.loop(GATHER_FAR, CHUNKS)
            def _(k):
                go_side(p, k, up_s, me).wait_recv()
                relay(p, k, go_side)

        at_distance(d, act)

    def ready(p):
        @pl.loop(0, GATHER_FAR)
        def _(k):
            go_y(p, k).wait_recv()

        go_c(p, 1).start()
        go_c(p, 0).wait_recv()
        go_c(p, 1).wait_recv()

    def plane(s):
        near = jnp.minimum(z, nz - 1 - z)
        step = lax.div(s + 1, 2)
        both = jnp.where(lax.rem(s, 2) == 1, z - step, z + step)
        far = jnp.where(z * 2 < nz, s, nz - 1 - s)
        return jnp.where(s <= 2 * near, both, far)

    def share(p, j, t):
        cols = pl.ds(pl.multiple_of(t * tile, tile), tile)
        return remote(
            sc.at[p, j, :, cols], rc.at[p, j, :, cols], rc_s.at[p, j, t], rc_r.at[p, j, t], peer_c
        )

    def share_y(p, k):
        return remote(
            sy.at[p, span(k)], ry.at[p, span(k)], ry_s.at[p, k], ry_r.at[p, k], peer_y
        )

    def share_z(way, p, at):
        landing = jnp.where((way == 1) & (z - 1 == p), nz, p)
        return remote(
            sz.at[p, span(at)], rz.at[landing, span(at)], rz_s.at[p, at], rz_r.at[landing, at],
            jnp.where(way == 0, me + 4, me - 4),
        )

    def land_z(slot, at):
        return remote(
            rz.at[slot, span(at)], rz.at[slot, span(at)], rz_s.at[0, at], rz_r.at[slot, at], me
        )

    hooks = units // wide + 1
    per = -(-CHUNKS // hooks)

    def compute(p, hook, middle):
        x = xs.at[p]
        cold_c = jnp.concatenate([column(cs[p * 4 + j, 0:1, :]) for j in range(4)], axis=0)

        @pl.loop(0, units // wide)
        def _(k):
            cols = pl.ds(pl.multiple_of(k * wide, wide), wide)
            v = x[...].reshape(4 * rows, model)
            g = jnp.dot(v, wg[:, cols], preferred_element_type=jnp.float32)
            u = jnp.dot(v, wu[:, cols], preferred_element_type=jnp.float32)
            hid[:, cols] = (g / (1.0 + jnp.exp(-g)) * u).astype(jnp.bfloat16)
            hook(k)

        v = x[...].reshape(4 * rows, model)
        gu = lax.dot_general(
            v, wh[: 2 * pad, :], (((1,), (1,)), ((), ())), preferred_element_type=jnp.float32
        )
        g, u = gu[:, :pad], gu[:, pad:]
        lane = lax.broadcasted_iota(jnp.int32, (rows, pad), 1)
        warm = []
        for j in range(4):
            scale = jnp.zeros((rows, pad), jnp.float32)
            for h in range(hot):
                weight = column(cs[p * 4 + j, 1 + h : 2 + h, :])
                scale = jnp.where((lane >= h * part) & (lane < (h + 1) * part), weight, scale)
            warm.append(scale)
        warm = jnp.concatenate(warm, axis=0)
        hhid[...] = (g / (1.0 + jnp.exp(-g)) * u * warm).astype(jnp.bfloat16)
        hook(hooks - 1)
        middle()

        @pl.loop(0, tiles)
        def _(t):
            cols = pl.ds(pl.multiple_of(t * tile, tile), tile)
            r = jnp.dot(hid[...], wd[:, cols], preferred_element_type=jnp.float32)
            r = r.astype(jnp.bfloat16).astype(jnp.float32) * cold_c
            r = r + jnp.dot(hhid[...], wh[2 * pad :, cols], preferred_element_type=jnp.float32)
            for j in range(2):
                low = r[2 * j * rows : (2 * j + 1) * rows]
                high = r[(2 * j + 1) * rows : (2 * j + 2) * rows]
                keep[p, j, :, cols] = jnp.where(c == 0, low, high)
                sc[p, j, :, cols] = jnp.where(c == 0, high, low).astype(jnp.bfloat16)
            share(p, 0, t).start()
            share(p, 1, t).start()

    def both_cores(p, j, k):
        return keep[p, j, span(k), :] + rc[p, j, span(k), :].astype(jnp.float32)

    def cross(p):
        @pl.loop(0, tiles)
        def _(t):
            share(p, 0, t).wait_recv()
            share(p, 1, t).wait_recv()

        @pl.loop(0, REDUCE_NEAR)
        def _(k):
            sy[p, span(k), :] = both_cores(p, 1 - y, k).astype(jnp.bfloat16)
            share_y(p, k).start()

    def onward(way, p, fed, at, total):
        value = total()
        if fed:
            land_z(p, at).wait_recv()
            value = value + rz[p, span(at), :].astype(jnp.float32)
        sz[p, span(at), :] = value.astype(jnp.bfloat16)
        share_z(way, p, at).start()

    def far_side(way, p, fed, k):
        onward(way, p, fed, CHUNKS + k - REDUCE_NEAR, lambda: both_cores(p, 1 - y, k))

    def far_own(way, p, fed, k):
        onward(way, p, fed, k, lambda: both_cores(p, y, k))

    def near_own(way, p, fed, k):
        share_y(p, k).wait_recv()
        onward(
            way, p, fed, k,
            lambda: both_cores(p, y, k) + ry[p, span(k), :].astype(jnp.float32),
        )

    out_way = jnp.where(z == 0, 0, 1)

    def send_far(p):
        @pl.loop(REDUCE_NEAR, CHUNKS)
        def _(k):
            far_side(out_way, p, False, k)
            far_own(out_way, p, False, k)

    def send_near(p):
        @pl.loop(0, REDUCE_NEAR)
        def _(k):
            near_own(out_way, p, False, k)

    def forward(hop):
        def ways(act):
            @pl.loop(0, 2)
            def _(turn):
                way = jnp.where(z * 2 < nz, turn, 1 - turn)
                p = jnp.where(way == 0, hop, nz - 1 - hop)
                active = jnp.where(way == 0, z < hop, z > nz - 1 - hop)

                @pl.when(active)
                def _():
                    act(way, p)

        @pl.loop(REDUCE_NEAR, CHUNKS)
        def _(k):
            def act(way, p):
                far_side(way, p, True, k)
                far_own(way, p, True, k)
            ways(act)

        @pl.loop(0, REDUCE_NEAR)
        def _(k):
            ways(lambda way, p: near_own(way, p, True, k))

    def arrived(j, k, at):
        keep[z, j, span(k), :] = both_cores(z, j, k)

        @pl.when(z > 0)
        def _():
            land_z(z, at).wait_recv()
            keep[z, j, span(k), :] += rz[z, span(at), :].astype(jnp.float32)

        @pl.when(z < nz - 1)
        def _():
            land_z(nz, at).wait_recv()
            keep[z, j, span(k), :] += rz[nz, span(at), :].astype(jnp.float32)

    def finish_side():
        @pl.loop(REDUCE_NEAR, CHUNKS)
        def _(k):
            arrived(1 - y, k, CHUNKS + k - REDUCE_NEAR)
            sy[z, span(k), :] = keep[z, 1 - y, span(k), :].astype(jnp.bfloat16)
            share_y(z, k).start()

    def finish_own(low, high):
        @pl.loop(low, high)
        def _(k):
            arrived(y, k, k)
            share_y(z, k).wait_recv()
            out[span(k), :] = (
                keep[z, y, span(k), :] + ry[z, span(k), :].astype(jnp.float32)
            ).astype(jnp.bfloat16)

    first.wait()

    @pl.loop(GATHER_FAR, CHUNKS)
    def _(k):
        go_y(z, k).start()

    @pl.loop(0, CHUNKS)
    def _(k):
        relay(z, k, go_own)

    @pl.loop(0, GATHER_FAR)
    def _(k):
        go_y(z, k).start()

    go_c(z, 0).start()

    @pl.loop(1, n)
    def _(i):
        ct_copy(i).start()

    @pl.loop(GATHER_FAR, CHUNKS)
    def _(k):
        go_y(z, k).wait_recv()
        relay(z, k, go_side)

    @pl.loop(0, CHUNKS)
    def _(k):
        serve_own(1, k)

    for load in loads:
        load.wait()

    @pl.loop(1, n)
    def _(i):
        other = lax.rem(me + i, n)
        remote(ct.at[other], cs.at[other], cts.at[i], ctr.at[other], other).wait_recv()

    ready(z)
    compute(z, lambda i: None, lambda: serve_side(1))
    cross(z)

    @pl.loop(1, nz)
    def _(s):
        p = plane(s)
        ready(p)

        def hook(i):
            @pl.loop(i * per, jnp.minimum(CHUNKS, (i + 1) * per))
            def _(k):
                serve_own(s + 1, k)

        def middle():
            serve_side(s + 1)

            @pl.when(corner & (s >= 2))
            def _():
                send_near(plane(s - 1))

        compute(p, hook, middle)
        cross(p)

        @pl.when(corner)
        def _():
            send_far(p)

    @pl.when(corner)
    def _():
        send_near(plane(nz - 1))
        finish_side()

    @pl.when(jnp.logical_not(corner))
    def _():
        for hop in range(2, nz):
            if hop == nz - 1:
                finish_side()
            forward(hop)

    finish_own(0, CHUNKS)

    @pl.loop(1, n)
    def _(i):
        ct_copy(i).wait_send()

    @pl.loop(0, nz)
    def _(p):
        def sent(k, go):
            @pl.when((p <= z) & (z + 1 < nz))
            def _():
                go(p, k, up_s, me + 4).wait_send()

            @pl.when((p >= z) & (z > 0))
            def _():
                go(p, k, down_s, me - 4).wait_send()

        @pl.loop(0, CHUNKS)
        def _(k):
            sent(k, go_own)

            @pl.when((k < GATHER_FAR) | (p == z))
            def _():
                go_y(p, k).wait_send()

            @pl.when(k >= GATHER_FAR)
            def _():
                sent(k, go_side)

            @pl.when((k < REDUCE_NEAR) | (p == z))
            def _():
                share_y(p, k).wait_send()

        go_c(p, 0).wait_send()
        go_c(p, 1).wait_send()

        @pl.loop(0, tiles)
        def _(t):
            share(p, 0, t).wait_send()
            share(p, 1, t).wait_send()

        @pl.when(p != z)
        def _():
            @pl.loop(0, 2 * CHUNKS - REDUCE_NEAR)
            def _(at):
                share_z(jnp.where(p > z, 0, 1), p, at).wait_send()


def scratch(n, rows, model, units, pad, hot):
    nz = n // 4
    half, full = jnp.bfloat16, jnp.float32
    dma = pltpu.SemaphoreType.DMA
    piece = rows // CHUNKS
    gathers, reduces = 2 * CHUNKS - GATHER_FAR, 2 * CHUNKS - REDUCE_NEAR
    tiles = model // tile_of(model, 512)
    return [
        pltpu.VMEM((nz, 4, rows, model), half),
        pltpu.VMEM((nz, 2, rows, model), full),
        pltpu.VMEM((nz, 2, rows, model), half),
        pltpu.VMEM((nz, 2, rows, model), half),
        pltpu.VMEM((nz, rows, model), half),
        pltpu.VMEM((nz, rows, model), half),
        pltpu.VMEM((nz, reduces * piece, model), half),
        pltpu.VMEM((nz + 1, reduces * piece, model), half),
        pltpu.VMEM((model, units), half),
        pltpu.VMEM((model, units), half),
        pltpu.VMEM((units, model), half),
        pltpu.VMEM((3 * pad, model), half),
        pltpu.VMEM((4 * rows, units), half),
        pltpu.VMEM((4 * rows, pad), half),
        pltpu.VMEM((n, 8, rows), full),
        pltpu.VMEM((n, 8, rows), full),
        dma((3 + 3 * hot,)), dma, dma((n,)), dma((n,)),
        dma((nz, gathers)), dma((nz, gathers)), dma((nz, gathers)),
        dma((nz, CHUNKS)), dma((nz, CHUNKS)), dma((nz, 2)), dma((nz, 2)),
        dma((nz, 2, tiles)), dma((nz, 2, tiles)),
        dma((nz, CHUNKS)), dma((nz, CHUNKS)),
        dma((nz, reduces)), dma((nz + 1, reduces)),
    ]


def shards(tokens, w_gate, w_up, w_down, hot_gate, hot_up, hot_down, cold_routes, hot_pick, gates):
    n = lax.axis_size("expert")
    micro_count, local_tokens, model = tokens.shape
    rows = micro_count * local_tokens
    hot, units, part = hot_gate.shape[0], w_gate.shape[2], hot_gate.shape[2]
    pad = -(-hot * part // 128) * 128
    need = rows * model * n * 9 // 2 * 2 + 3 * model * (units + pad) * 2
    if n % 4 or part % 16 or rows % 64 or model % 256 or need > ROOM or hot > 7:
        return routed(
            tokens, w_gate, w_up, w_down, hot_gate, hot_up, hot_down, cold_routes, hot_pick, gates
        )
    anyplace = pl.BlockSpec(memory_space=pl.ANY)
    vmem = pl.BlockSpec(memory_space=pltpu.VMEM)
    mixed = pl.pallas_call(
        functools.partial(fused, n, hot, part),
        out_shape=jax.ShapeDtypeStruct((rows, model), jnp.bfloat16),
        in_specs=[anyplace, vmem, vmem, vmem] + [anyplace] * 6,
        out_specs=vmem,
        scratch_shapes=scratch(n, rows, model, units, pad, hot),
        compiler_params=pltpu.CompilerParams(
            collective_id=0, has_side_effects=True, vmem_limit_bytes=64 * 2**20 - 2**17
        ),
    )(
        tokens.reshape(rows, model), jnp.transpose(cold_routes, (2, 0, 1)), hot_pick,
        jnp.swapaxes(gates, 1, 2),
        w_gate[0], w_up[0], w_down[0],
        *(jnp.swapaxes(w, 1, 2) for w in (hot_gate, hot_up, hot_down)),
    )
    return mixed.reshape(tokens.shape)


def solution(mesh):
    in_specs = (
        P(None, ("groups", "expert"), None),
        P("expert", None, None),
        P("expert", None, None),
        P("expert", None, None),
        P(None, None, "expert"),
        P(None, None, "expert"),
        P(None, None, "expert"),
        P(None, ("groups", "expert"), None),
        P(None, ("groups", "expert")),
        P(None, ("groups", "expert"), None),
    )
    out_specs = P(None, ("groups", "expert"), None)
    return jax.shard_map(shards, mesh=mesh, in_specs=in_specs, out_specs=out_specs, check_vma=False)
```

```python
import functools

import jax
import jax.numpy as jnp
from jax import lax
from jax.experimental import pallas as pl
from jax.experimental.pallas import tpu as pltpu
from jax.sharding import PartitionSpec as P

TOP = 8
HOT = 2


def expert_rows(rows_in, weights):
    leading = rows_in.shape[:-1]
    flat_rows = rows_in.reshape(-1, rows_in.shape[-1])
    gate = jnp.dot(flat_rows, weights[0], preferred_element_type=jnp.float32)
    upward = jnp.dot(flat_rows, weights[1], preferred_element_type=jnp.float32)
    hidden = (jax.nn.silu(gate) * upward).astype(jnp.bfloat16)
    result = jnp.dot(hidden, weights[2], preferred_element_type=jnp.float32).astype(jnp.bfloat16)
    return result.reshape(leading + (result.shape[-1],))


def slot_table(routes_block, axis_width, capacity):
    expert = routes_block.reshape(-1)
    total_count = expert.shape[0]
    onehot = (expert[:, None] == jnp.arange(axis_width, dtype=jnp.int32)[None, :]).astype(jnp.int32)
    before = jnp.cumsum(onehot, axis=0) - onehot
    slot_rank = jnp.sum(before * onehot, axis=1)
    slot_place = expert * capacity + slot_rank
    target = jnp.arange(axis_width * capacity, dtype=jnp.int32)
    matched = slot_place[None, :] == target[:, None]
    filled = jnp.any(matched, axis=1)
    source = jnp.sum(
        jnp.where(matched, jnp.arange(total_count, dtype=jnp.int32)[None, :], 0), axis=1
    )
    return (slot_place, source, filled)


def routed(tokens, w_gate, w_up, w_down, hot_gate, hot_up, hot_down, cold_routes, hot_pick, gates):
    axis_width = lax.axis_size("expert")
    micro_count, local_tokens, model_width = tokens.shape
    picks = TOP - 1
    capacity = local_tokens * picks * 3 // (2 * axis_width) + 1
    own_weights = (w_gate[0], w_up[0], w_down[0])
    outbound = []
    tables = []
    for micro in range(micro_count):
        slot_place, source, filled = slot_table(cold_routes[micro], axis_width, capacity)
        rows_out = tokens[micro][source // picks]
        rows_out = jnp.where(filled[:, None], rows_out, jnp.zeros_like(rows_out))
        outbound.append(rows_out.reshape(axis_width, capacity, model_width))
        tables.append(slot_place)
    joined = jnp.concatenate(outbound, axis=1)
    back_all = lax.all_to_all(
        expert_rows(
            lax.all_to_all(joined, "expert", split_axis=0, concat_axis=0, tiled=True), own_weights
        ),
        "expert",
        split_axis=0,
        concat_axis=0,
        tiled=True,
    )
    returned = [
        back_all[:, micro * capacity : (micro + 1) * capacity] for micro in range(micro_count)
    ]
    cold_parts = []
    for micro in range(micro_count):
        picked = returned[micro].reshape(axis_width * capacity, model_width)[tables[micro]]
        picked = picked.reshape(local_tokens, picks, model_width).astype(jnp.float32)
        cold_parts.append(jnp.sum(picked * gates[micro, :, 1:, None], axis=1))
    cold_total = jnp.stack(cold_parts)
    all_rows = micro_count * local_tokens
    flat = tokens.reshape(all_rows, model_width)
    order = jnp.argsort(hot_pick.reshape(all_rows), stable=True)
    share = all_rows // HOT
    grouped = flat[order].reshape(HOT, share, model_width)
    gate = jnp.einsum(
        "hsd,hdf->hsf",
        grouped,
        lax.all_gather(hot_gate, "expert", axis=2, tiled=True),
        preferred_element_type=jnp.float32,
    )
    upward = jnp.einsum(
        "hsd,hdf->hsf",
        grouped,
        lax.all_gather(hot_up, "expert", axis=2, tiled=True),
        preferred_element_type=jnp.float32,
    )
    hidden = (jax.nn.silu(gate) * upward).astype(jnp.bfloat16)
    hot_sum = jnp.einsum(
        "hsf,hdf->hsd",
        hidden,
        lax.all_gather(hot_down, "expert", axis=2, tiled=True),
        preferred_element_type=jnp.float32,
    )
    sorted_out = hot_sum.astype(jnp.bfloat16).reshape(all_rows, model_width)
    inverse = jnp.argsort(order)
    hot_out = sorted_out[inverse].astype(jnp.float32) * gates[:, :, 0].reshape(all_rows)[:, None]
    total = hot_out.reshape(micro_count, local_tokens, model_width) + cold_total
    return total.astype(jnp.bfloat16)


(
    CROSS_FIRST, SEND_Z, SEND_Y, SEND_CORE, PASS_Z, PASS_CORE, RELAY_OWN, RELAY_SIDE,
    RELAY_CORE, CROSS, REDUCE_SIDE, REDUCE_FAR, REDUCE_NEAR, FINISH_SIDE, FINISH_OWN, STEP,
) = range(16)
OWN, SIDE, FROM_Y, CORE_OWN, CORE_SIDE, SHARE_OWN, SHARE_SIDE, SUM_Y, SUM_Z = range(9)
AHEAD, BEHIND = range(2)
CHUNKS = 8
NEAR_IN = 7
NEAR_OUT = 4
HIGH = (5, 4, 6, 7)
LOW = (3, 2, 0, 1)
STEPS = 6
UNITS = (
    ((2, 0), (1, 0), (3, 0), (0, 1), (3, 1), (2, 1), (1, 1), (0, 0)),
    ((0, 0), (1, 1), (2, 0), (0, 1), (1, 0), (3, 0), (3, 1), (2, 1)),
)
OUTER = (
    (SEND_Z, 6, AHEAD), (SEND_CORE,), (SEND_Y, 6), (CROSS_FIRST,), (SEND_Z, 7, AHEAD),
    (SEND_Z, 4, AHEAD), (SEND_Y, 2), (RELAY_OWN, 1, 5), (SEND_Y, 1), (SEND_Z, 5, AHEAD),
    (PASS_CORE, 6), (SEND_Z, 2, AHEAD), (SEND_Z, 1, AHEAD), (PASS_Z, 7), (SEND_Z, 3, AHEAD),
    (PASS_CORE, 7), (RELAY_OWN, 1, 4), (PASS_CORE, 2), (RELAY_OWN, 2, 7), (RELAY_CORE, 1, 5),
    (RELAY_OWN, 2, 4), (PASS_CORE, 1), (RELAY_SIDE, 1, 7), (RELAY_CORE, 1, 4), (RELAY_OWN, 2, 5),
    (SEND_Z, 0, AHEAD), (RELAY_CORE, 2, 4), (RELAY_OWN, 2, 6), (SEND_Y, 0), (RELAY_SIDE, 2, 7),
    (RELAY_CORE, 2, 5), (RELAY_OWN, 3, 7), (RELAY_CORE, 2, 6), (STEP, 0, 0), (RELAY_OWN, 2, 0),
    (PASS_CORE, 0), (RELAY_OWN, 1, 6), (STEP, 0, 1), (STEP, 0, 2), (RELAY_OWN, 3, 4),
    (STEP, 0, 3), (STEP, 0, 4), (RELAY_OWN, 3, 6), (STEP, 0, 5), (RELAY_CORE, 2, 0),
    (RELAY_CORE, 1, 6), (SEND_Y, 5), (RELAY_OWN, 3, 5), (RELAY_OWN, 1, 0), (REDUCE_FAR, 2, 4),
    (REDUCE_FAR, 2, 6), (REDUCE_FAR, 2, 5), (REDUCE_FAR, 2, 7), (REDUCE_SIDE, 2, 7),
    (REDUCE_SIDE, 2, 5), (REDUCE_SIDE, 2, 4), (RELAY_CORE, 3, 4), (REDUCE_SIDE, 2, 6),
    (RELAY_OWN, 1, 7), (RELAY_CORE, 3, 6), (STEP, 1, 0), (RELAY_OWN, 2, 3), (STEP, 1, 1),
    (PASS_CORE, 5), (RELAY_OWN, 3, 1), (STEP, 1, 2), (RELAY_CORE, 3, 5), (RELAY_SIDE, 3, 7),
    (STEP, 1, 3), (STEP, 1, 4), (RELAY_CORE, 1, 0), (SEND_Y, 3), (RELAY_OWN, 3, 3), (STEP, 1, 5),
    (STEP, 2, 0), (RELAY_CORE, 2, 3), (RELAY_OWN, 2, 1), (REDUCE_FAR, 1, 6), (STEP, 2, 1),
    (RELAY_OWN, 1, 1), (RELAY_CORE, 3, 1), (REDUCE_SIDE, 1, 6), (STEP, 2, 2), (PASS_CORE, 3),
    (STEP, 2, 3), (STEP, 2, 4), (RELAY_CORE, 3, 3), (STEP, 2, 5), (RELAY_OWN, 3, 2), (STEP, 3, 0),
    (RELAY_OWN, 3, 0), (REDUCE_FAR, 3, 6), (REDUCE_FAR, 3, 5), (RELAY_CORE, 2, 1),
    (REDUCE_FAR, 3, 4), (REDUCE_SIDE, 3, 7), (REDUCE_SIDE, 3, 6), (REDUCE_SIDE, 3, 4),
    (STEP, 3, 1), (RELAY_OWN, 1, 3), (RELAY_CORE, 1, 1), (STEP, 3, 2), (RELAY_OWN, 2, 2),
    (SEND_Y, 4), (STEP, 3, 3), (STEP, 3, 4), (RELAY_CORE, 3, 0), (STEP, 3, 5), (REDUCE_FAR, 1, 4),
    (RELAY_OWN, 1, 2), (REDUCE_FAR, 1, 5), (RELAY_CORE, 1, 3), (REDUCE_SIDE, 1, 5),
    (REDUCE_FAR, 1, 7), (REDUCE_SIDE, 1, 7), (REDUCE_SIDE, 1, 4), (REDUCE_SIDE, 3, 5),
    (REDUCE_FAR, 3, 7), (RELAY_CORE, 3, 2), (CROSS, 0, 3), (CROSS, 0, 1), (CROSS, 0, 0),
    (CROSS, 0, 2), (RELAY_CORE, 2, 2), (STEP, 4, 0), (STEP, 4, 1), (STEP, 4, 2),
    (RELAY_CORE, 1, 2), (STEP, 4, 3), (STEP, 4, 4), (STEP, 4, 5), (STEP, 5, 0), (STEP, 5, 1),
    (CROSS, 3, 2), (CROSS, 3, 0), (CROSS, 3, 1), (STEP, 5, 2), (STEP, 5, 3), (STEP, 5, 4),
    (STEP, 5, 5), (REDUCE_NEAR, 3, 2), (STEP, 6, 0), (STEP, 6, 1), (CROSS, 2, 3), (CROSS, 2, 0),
    (CROSS, 2, 2), (REDUCE_NEAR, 3, 0), (STEP, 6, 2), (REDUCE_NEAR, 3, 1), (STEP, 6, 3),
    (STEP, 6, 4), (STEP, 6, 5), (REDUCE_NEAR, 2, 3), (CROSS, 3, 3), (CROSS, 2, 1), (PASS_CORE, 4),
    (REDUCE_NEAR, 2, 0), (CROSS, 1, 1), (CROSS, 1, 3), (CROSS, 1, 2), (STEP, 7, 0), (STEP, 7, 1),
    (STEP, 7, 2), (REDUCE_NEAR, 3, 3), (STEP, 7, 3), (STEP, 7, 4), (REDUCE_NEAR, 2, 1),
    (STEP, 7, 5), (REDUCE_NEAR, 2, 2), (CROSS, 1, 0), (REDUCE_NEAR, 1, 1), (FINISH_SIDE, 0, 7),
    (FINISH_SIDE, 0, 6), (FINISH_SIDE, 0, 4), (REDUCE_NEAR, 1, 3), (FINISH_SIDE, 0, 5),
    (REDUCE_NEAR, 1, 2), (REDUCE_NEAR, 1, 0), (FINISH_OWN, 0, 0), (FINISH_OWN, 0, 7),
    (FINISH_OWN, 0, 1), (FINISH_OWN, 0, 6), (FINISH_OWN, 0, 2), (FINISH_OWN, 0, 4),
    (FINISH_OWN, 0, 3), (FINISH_OWN, 0, 5),
)
INNER = (
    (SEND_Y, 1), (SEND_Z, 7, AHEAD), (SEND_Z, 5, BEHIND), (SEND_Y, 3), (CROSS_FIRST,),
    (SEND_Z, 6, BEHIND), (SEND_Z, 4, AHEAD), (SEND_Y, 2), (SEND_Z, 6, AHEAD), (SEND_Z, 4, BEHIND),
    (SEND_CORE,), (PASS_CORE, 1), (SEND_Z, 5, AHEAD), (RELAY_OWN, 2, 7), (RELAY_OWN, 0, 6),
    (PASS_CORE, 3), (RELAY_OWN, 2, 4), (SEND_Y, 5), (PASS_CORE, 7), (PASS_Z, 7),
    (RELAY_OWN, 0, 7), (SEND_Z, 0, AHEAD), (RELAY_OWN, 0, 4), (PASS_CORE, 2), (RELAY_OWN, 2, 5),
    (RELAY_OWN, 0, 5), (RELAY_CORE, 0, 6), (RELAY_OWN, 0, 2), (SEND_Y, 0), (RELAY_OWN, 2, 6),
    (RELAY_CORE, 2, 4), (SEND_Z, 3, AHEAD), (RELAY_OWN, 0, 1), (RELAY_SIDE, 2, 7), (PASS_CORE, 5),
    (RELAY_OWN, 3, 7), (RELAY_SIDE, 0, 7), (RELAY_CORE, 0, 4), (RELAY_OWN, 2, 0),
    (SEND_Z, 0, BEHIND), (RELAY_OWN, 0, 3), (RELAY_CORE, 2, 5), (SEND_Y, 4), (RELAY_OWN, 0, 0),
    (RELAY_OWN, 3, 4), (RELAY_OWN, 3, 6), (RELAY_CORE, 0, 5), (SEND_Z, 1, AHEAD), (STEP, 0, 0),
    (RELAY_OWN, 3, 5), (RELAY_CORE, 0, 2), (SEND_Z, 7, BEHIND), (STEP, 0, 1), (PASS_CORE, 0),
    (RELAY_OWN, 2, 3), (STEP, 0, 2), (RELAY_OWN, 3, 1), (SEND_Y, 6), (STEP, 0, 3), (STEP, 0, 4),
    (STEP, 0, 5), (RELAY_CORE, 0, 1), (RELAY_SIDE, 3, 7), (STEP, 1, 0), (RELAY_OWN, 3, 3),
    (RELAY_CORE, 2, 0), (STEP, 1, 1), (RELAY_CORE, 0, 3), (STEP, 1, 2), (STEP, 1, 3),
    (RELAY_OWN, 2, 1), (SEND_Z, 1, BEHIND), (STEP, 1, 4), (STEP, 1, 5), (RELAY_CORE, 2, 6),
    (PASS_CORE, 4), (SEND_Z, 2, AHEAD), (SEND_Z, 2, BEHIND), (RELAY_CORE, 0, 0),
    (RELAY_OWN, 3, 2), (RELAY_OWN, 3, 0), (SEND_Z, 3, BEHIND), (RELAY_CORE, 3, 4), (CROSS, 1, 3),
    (CROSS, 1, 2), (CROSS, 1, 0), (STEP, 2, 0), (RELAY_CORE, 3, 6), (STEP, 2, 1),
    (RELAY_OWN, 2, 2), (STEP, 2, 2), (RELAY_CORE, 3, 5), (STEP, 2, 3), (RELAY_CORE, 2, 3),
    (STEP, 2, 4), (STEP, 2, 5), (RELAY_CORE, 3, 1), (STEP, 3, 0), (STEP, 3, 1),
    (REDUCE_SIDE, 2, 6), (PASS_CORE, 6), (REDUCE_FAR, 2, 5), (REDUCE_FAR, 2, 6),
    (REDUCE_FAR, 2, 4), (REDUCE_SIDE, 2, 5), (REDUCE_SIDE, 2, 4), (STEP, 3, 2),
    (RELAY_CORE, 3, 3), (STEP, 3, 3), (STEP, 3, 4), (RELAY_CORE, 2, 1), (STEP, 3, 5),
    (STEP, 4, 0), (STEP, 4, 1), (RELAY_CORE, 3, 0), (CROSS, 0, 0), (STEP, 4, 2), (STEP, 4, 3),
    (STEP, 4, 4), (STEP, 4, 5), (STEP, 5, 0), (STEP, 5, 1), (FINISH_SIDE, 1, 6), (STEP, 5, 2),
    (STEP, 5, 3), (STEP, 5, 4), (STEP, 5, 5), (RELAY_CORE, 2, 2), (REDUCE_FAR, 2, 7),
    (FINISH_OWN, 1, 6), (CROSS, 0, 3), (RELAY_CORE, 3, 2), (CROSS, 0, 1), (CROSS, 1, 1),
    (REDUCE_SIDE, 2, 7), (CROSS, 0, 2), (REDUCE_FAR, 3, 5), (REDUCE_FAR, 3, 6),
    (REDUCE_FAR, 3, 4), (REDUCE_SIDE, 3, 4), (REDUCE_SIDE, 3, 6), (REDUCE_SIDE, 3, 7),
    (STEP, 6, 0), (FINISH_SIDE, 1, 5), (STEP, 6, 1), (STEP, 6, 2), (STEP, 6, 3),
    (FINISH_SIDE, 1, 7), (STEP, 6, 4), (REDUCE_FAR, 0, 5), (STEP, 6, 5), (STEP, 7, 0),
    (REDUCE_FAR, 0, 6), (REDUCE_SIDE, 3, 5), (STEP, 7, 1), (CROSS, 3, 0), (REDUCE_FAR, 0, 4),
    (CROSS, 3, 1), (REDUCE_FAR, 3, 7), (CROSS, 3, 3), (CROSS, 3, 2), (STEP, 7, 2), (STEP, 7, 3),
    (STEP, 7, 4), (REDUCE_SIDE, 0, 6), (STEP, 7, 5), (REDUCE_NEAR, 3, 0), (REDUCE_SIDE, 0, 4),
    (FINISH_OWN, 1, 7), (FINISH_OWN, 1, 5), (FINISH_SIDE, 1, 4), (REDUCE_SIDE, 0, 7),
    (REDUCE_NEAR, 3, 1), (CROSS, 2, 1), (CROSS, 2, 0), (CROSS, 2, 3), (CROSS, 2, 2),
    (REDUCE_SIDE, 0, 5), (REDUCE_FAR, 0, 7), (REDUCE_NEAR, 3, 2), (REDUCE_NEAR, 0, 0),
    (REDUCE_NEAR, 3, 3), (FINISH_OWN, 1, 4), (REDUCE_NEAR, 0, 1), (REDUCE_NEAR, 2, 1),
    (REDUCE_NEAR, 0, 2), (REDUCE_NEAR, 2, 0), (REDUCE_NEAR, 0, 3), (REDUCE_NEAR, 2, 3),
    (FINISH_OWN, 1, 1), (REDUCE_NEAR, 2, 2), (FINISH_OWN, 1, 3), (FINISH_OWN, 1, 0),
    (FINISH_OWN, 1, 2),
)
ROOM = 56 * 2**20


def tile_of(extent, most):
    return most if extent % most == 0 else extent


def needs(q, nz, task):
    name, *at = task
    if name in (CROSS_FIRST, SEND_Z, SEND_Y, SEND_CORE):
        return []
    if name in (PASS_Z, PASS_CORE):
        return [(FROM_Y, q, at[0])]
    p, k = at
    if name == RELAY_OWN:
        return [(OWN, p, k)]
    if name == RELAY_SIDE:
        return [(SIDE, p, k)]
    if name == RELAY_CORE:
        return [(FROM_Y, p, k)]
    h = 0 if k >= CHUNKS // 2 else 1
    own, side = ([(share, p, h, t) for t in range(2)] for share in (SHARE_OWN, SHARE_SIDE))
    if p == q:
        came = [w for w, there in ((AHEAD, q > 0), (BEHIND, q < nz - 1)) if there]
    else:
        came = [w for w, there in ((AHEAD, p > q > 0), (BEHIND, p < q < nz - 1)) if there]
    far = [(SUM_Z, p, CHUNKS + k - NEAR_OUT, w) for w in came]
    mine = [(SUM_Z, p, k, w) for w in came]
    cross = [(SUM_Y, p, k)]
    return {
        CROSS: side, REDUCE_SIDE: side + far, FINISH_SIDE: side + far,
        REDUCE_FAR: own + mine, REDUCE_NEAR: own + cross + mine, FINISH_OWN: own + cross + mine,
    }[name]


def hooks(q, nz, tasks):
    at, waited = (-1, STEPS - 1), set()
    plan = {at: []}

    def fresh(keys):
        news = [key for key in keys if key not in waited]
        waited.update(news)
        return news

    for task in tasks:
        if task[0] != STEP:
            plan[at].append((fresh(needs(q, nz, task)), task))
            continue
        if task[2] == 0:
            p, h = UNITS[q][task[1]]
            half = range(CHUNKS // 2, CHUNKS) if h == 0 else range(CHUNKS // 2)
            keys = [(core, p, k) for core in (CORE_OWN, CORE_SIDE) for k in half]
            keys += [(FROM_Y, p, k) for k in half if p == q or k < NEAR_IN]
            if p != q:
                keys += [(OWN, p, k) for k in half]
                keys += [(SIDE, p, k) for k in half if k >= NEAR_IN]
            plan[at].append((fresh(keys), None))
        at = (task[1], task[2])
        plan[at] = []
    return plan


def fused(
    n, hot, part, tok, routes, pick, gts, wg_in, wu_in, wd_in, hg_in, hu_in, hd_in, out,
    xs, keep, sc, rc, sy, ry, sz, rz, wg, wu, wd, wh, hid, hhid, cs, ct, gw,
    wsem, tsem, cts, ctr, up_s, down_s, z_r, y_s, y_r, c_s, c_r,
    rc_s, rc_r, ry_s, ry_r, rz_s, rz_r,
):
    nz = n // 4
    rows, model = tok.shape
    units = wg.shape[1]
    pad = hhid.shape[1]
    piece = rows // CHUNKS
    half = rows // 2
    wide = units // 3
    band = model // 2
    tile = tile_of(band, 512)
    me = lax.axis_index("expert")
    c = lax.rem(me, 2)
    y = lax.rem(lax.div(me, 2), 2)
    z = lax.div(me, 4)
    own = y * 2 + c
    side = (1 - y) * 2 + c
    peer_y = z * 4 + side
    peer_c = z * 4 + y * 2 + (1 - c)
    outer = (z == 0) | (z == nz - 1)
    low = z * 2 < nz

    def plane(p):
        return jnp.where(low, p, nz - 1 - p)

    ahead = me + jnp.where(low, 4, -4)
    behind = me - jnp.where(low, 4, -4)

    def remote(src, dst, send, recv, device):
        return pltpu.make_async_remote_copy(
            src_ref=src, dst_ref=dst, send_sem=send, recv_sem=recv,
            device_id={"expert": device}, device_id_type=pl.DeviceIdType.MESH,
        )

    def span(k):
        return pl.ds(k * piece, piece)

    loads = [
        pltpu.make_async_copy(src, dst, wsem.at[i])
        for i, (src, dst) in enumerate((
            *(
                (src.at[h], wh.at[pl.ds(t * pad + h * part, part)])
                for t, src in enumerate((hg_in, hu_in, hd_in)) for h in range(hot)
            ),
            (wg_in, wg), (wu_in, wu), (wd_in, wd),
        ))
    ]
    first = pltpu.make_async_copy(tok, xs.at[z, own], tsem)
    first.start()
    barrier = pltpu.get_barrier_semaphore()

    @pl.loop(1, n)
    def _(i):
        pl.semaphore_signal(
            barrier, inc=1, device_id={"expert": lax.rem(me + i, n)},
            device_id_type=pl.DeviceIdType.MESH,
        )

    ct[...] = jnp.zeros_like(ct)
    micros = gts.shape[0]

    def joined(parts):
        return jnp.concatenate(parts, axis=1)

    warm_row = joined([gts[m, 0:1, :] for m in range(micros)])
    chosen = joined([pick[m : m + 1, :] for m in range(micros)])
    named = [
        (
            joined([routes[k, m : m + 1, :] for m in range(micros)]),
            joined([gts[m, k + 1 : k + 2, :] for m in range(micros)]),
        )
        for k in range(routes.shape[0])
    ]

    def row(e):
        return sum(jnp.where(route == e, weight, 0.0) for route, weight in named)

    for e in range(n):
        ct[e, 0:1, :] = row(e)
        for h in range(hot):
            ct[e, 1 + h : 2 + h, :] = jnp.where(chosen == h, warm_row, 0.0)

    cs[me] = ct[me]
    first.wait()
    for load in loads:
        load.start()
    pl.semaphore_wait(barrier, n - 1)

    def ct_copy(i):
        peer = lax.rem(me + i, n)
        return remote(ct.at[peer], cs.at[me], cts.at[i], ctr.at[me], peer)

    def go_z(way, p, slot, k):
        at = k if slot is own else CHUNKS + k - NEAR_IN
        ref = xs.at[plane(p), slot, span(k)]
        send = up_s if way == AHEAD else down_s
        return remote(
            ref, ref, send.at[plane(p), at], z_r.at[plane(p), at],
            ahead if way == AHEAD else behind,
        )

    def go_y(p, k):
        ref = xs.at[plane(p), own, span(k)]
        return remote(ref, ref, y_s.at[plane(p), k], y_r.at[plane(p), k], peer_y)

    def go_c(p, which, k):
        ref = xs.at[plane(p), (own, side)[which], span(k)]
        return remote(
            ref, ref, c_s.at[plane(p), which, k], c_r.at[plane(p), which, k], peer_c
        )

    def share(at, h, j, t):
        lines = pl.ds(pl.multiple_of((1 - h) * half, half), half)
        cols = pl.ds(t * band, band)
        return remote(
            sc.at[at, j, lines, cols], rc.at[at, j, lines, cols],
            rc_s.at[at, h, j, t], rc_r.at[at, h, j, t], peer_c,
        )

    def share_y(p, k):
        at = plane(p)
        return remote(
            sy.at[at, span(k)], ry.at[at, span(k)], ry_s.at[at, k], ry_r.at[at, k], peer_y
        )

    def landing(way, p, last):
        if not last:
            return plane(p)
        return jnp.where(low == (way == AHEAD), plane(p), nz)

    def share_z(way, q, p, at):
        slot = landing(way, p, p == (q + 1 if way == AHEAD else q - 1))
        return remote(
            sz.at[plane(p), span(at)], rz.at[slot, span(at)],
            rz_s.at[plane(p), at], rz_r.at[slot, at],
            ahead if way == AHEAD else behind,
        )

    def await_event(q, key):
        name, p, k, *rest = key
        if name == OWN:
            go_z(AHEAD, p, own, k).wait_recv()
        elif name == SIDE:
            go_z(AHEAD, p, side, k).wait_recv()
        elif name == FROM_Y:
            ref = xs.at[plane(p), side, span(k)]
            remote(ref, ref, y_s.at[plane(p), k], y_r.at[plane(p), k], peer_y).wait_recv()
        elif name in (CORE_OWN, CORE_SIDE):
            go_c(p, int(name == CORE_SIDE), k).wait_recv()
        elif name in (SHARE_OWN, SHARE_SIDE):
            share(plane(p), k, y if name == SHARE_OWN else 1 - y, rest[0]).wait_recv()
        elif name == SUM_Y:
            share_y(p, k).wait_recv()
        else:
            slot = landing(rest[0], p, p == q)
            ref = rz.at[slot, span(k)]
            remote(ref, ref, rz_s.at[0, k], rz_r.at[slot, k], me).wait_recv()

    def ways(q, p):
        return (AHEAD,) * (p <= q and q + 1 < nz) + (BEHIND,) * (p >= q and q > 0)

    def add_up(dst, lines, terms):
        @pl.loop(0, model // tile)
        def _(t):
            cols = pl.ds(pl.multiple_of(t * tile, tile), tile)
            total = None
            for term in terms:
                value = term(cols).astype(jnp.float32)
                total = value if total is None else total + value
            dst[lines, cols] = total.astype(jnp.bfloat16)

    def act(q, task):
        name, *at = task
        if name == CROSS_FIRST:
            for k in HIGH + LOW:
                if k >= NEAR_IN:
                    go_y(q, k).start()
        elif name == SEND_Z:
            go_z(at[1], q, own, at[0]).start()
        elif name == SEND_CORE:
            for k in range(CHUNKS):
                go_c(q, 0, k).start()
        elif name == PASS_Z:
            for way in ways(q, q):
                go_z(way, q, side, at[0]).start()
        elif name == SEND_Y:
            go_y(q, at[0]).start()
        elif name == PASS_CORE:
            go_c(q, 1, at[0]).start()
        elif name == RELAY_OWN:
            p, k = at
            for way in ways(q, p):
                go_z(way, p, own, k).start()
            if k < NEAR_IN:
                go_y(p, k).start()
            go_c(p, 0, k).start()
        elif name == RELAY_SIDE:
            p, k = at
            for way in ways(q, p):
                go_z(way, p, side, k).start()
            go_c(p, 1, k).start()
        elif name == RELAY_CORE:
            go_c(at[0], 1, at[1]).start()
        else:
            p, k = at
            j = 1 - y if name in (CROSS, REDUCE_SIDE, FINISH_SIDE) else y
            here = plane(p)
            terms = [
                lambda cols: keep[here, j, span(k), cols],
                lambda cols: rc[here, j, span(k), cols],
            ]
            for key in needs(q, nz, task):
                if key[0] == SUM_Y:
                    terms.append(lambda cols: ry[here, span(k), cols])
                if key[0] == SUM_Z:
                    slot, line = landing(key[3], p, p == q), span(key[2])
                    terms.append(lambda cols, slot=slot, line=line: rz[slot, line, cols])
            if name in (CROSS, FINISH_SIDE):
                add_up(sy.at[here], span(k), terms)
                share_y(p, k).start()
            elif name == FINISH_OWN:
                add_up(out, span(k), terms)
            else:
                line = CHUNKS + k - NEAR_OUT if name == REDUCE_SIDE else k
                add_up(sz.at[here], span(line), terms)
                share_z(AHEAD if p > q else BEHIND, q, p, line).start()

    plans = [hooks(q, nz, tasks) for q, tasks in enumerate((OUTER, INNER))]

    def perform(q, steps):
        for keys, task in steps:
            for key in keys:
                await_event(q, key)
            if task is not None:
                act(q, task)

    def by_class(emit):
        @pl.when(outer)
        def _():
            emit(0)

        @pl.when(jnp.logical_not(outer))
        def _():
            emit(1)

    count = len(UNITS[0])

    def hook(u, step):
        def emit(q):
            for j in range(count):
                if (j, step) != (count - 1, STEPS - 1) and plans[q].get((j, step)):
                    @pl.when(u == j)
                    def _():
                        perform(q, plans[q][j, step])

        by_class(emit)

    def picked(u, field):
        found = [
            functools.reduce(
                lambda rest, j: jnp.where(u == j, UNITS[q][j][field], rest),
                range(1, count), jnp.int32(UNITS[q][0][field]),
            )
            for q in range(2)
        ]
        return jnp.where(outer, *found)

    def take_tables():
        if pad > hot * part:
            for t in range(3):
                blank = wh.at[pl.ds(t * pad + hot * part, pad - hot * part)]
                blank[...] = jnp.zeros_like(blank)

        for load in loads:
            load.wait()

        @pl.loop(1, n)
        def _(i):
            other = lax.rem(me + i, n)
            remote(
                ct.at[other], cs.at[other], cts.at[i], ctr.at[other], other
            ).wait_recv()

        @pl.loop(0, n)
        def _(e):
            gw[e] = jnp.transpose(cs[e])

    def start(q):
        for keys, task in plans[q][-1, STEPS - 1]:
            if task is None:
                take_tables()
            perform(q, [(keys, task)])

    @pl.loop(1, n)
    def _(i):
        ct_copy(i).start()

    by_class(start)

    @pl.loop(0, count)
    def _(u):
        here = plane(picked(u, 0))
        h = picked(u, 1)
        lines = pl.ds(pl.multiple_of((1 - h) * half, half), half)

        def block():
            return xs[here, :, lines, :].reshape(4 * half, model)

        def columns(which):
            return jnp.concatenate(
                [gw[here * 4 + j, lines, which : which + 1] for j in range(4)], axis=0
            )

        for i in range(3):
            cols = pl.ds(i * wide, wide)
            v = block()
            g = jnp.dot(v, wg[:, cols], preferred_element_type=jnp.float32)
            up = jnp.dot(v, wu[:, cols], preferred_element_type=jnp.float32)
            hid[:, cols] = (g / (1.0 + jnp.exp(-g)) * up).astype(jnp.bfloat16)
            hook(u, i)

        gu = lax.dot_general(
            block(), wh[: 2 * pad, :], (((1,), (1,)), ((), ())),
            preferred_element_type=jnp.float32,
        )
        g, up = gu[:, :pad], gu[:, pad:]
        lane = lax.broadcasted_iota(jnp.int32, (4 * half, pad), 1)
        warm = jnp.zeros((4 * half, pad), jnp.float32)
        for i in range(hot):
            warm = jnp.where((lane >= i * part) & (lane < (i + 1) * part), columns(1 + i), warm)
        hhid[...] = (g / (1.0 + jnp.exp(-g)) * up * warm).astype(jnp.bfloat16)
        hook(u, 3)

        cold = columns(0)
        for t in range(2):
            for i in range(band // tile):
                cols = pl.ds(t * band + i * tile, tile)
                r = jnp.dot(hid[...], wd[:, cols], preferred_element_type=jnp.float32)
                r = r.astype(jnp.bfloat16).astype(jnp.float32) * cold
                r = r + jnp.dot(
                    hhid[...], wh[2 * pad :, cols], preferred_element_type=jnp.float32
                )
                for j in range(2):
                    even = r[2 * j * half : (2 * j + 1) * half]
                    odd = r[(2 * j + 1) * half : (2 * j + 2) * half]
                    keep[here, j, lines, cols] = jnp.where(c == 0, even, odd)
                    sc[here, j, lines, cols] = jnp.where(c == 0, odd, even).astype(jnp.bfloat16)
            share(here, h, 1 - y, t).start()
            share(here, h, y, t).start()
            hook(u, 4 + t)

    by_class(lambda q: perform(q, plans[q][count - 1, STEPS - 1]))

    @pl.loop(1, n)
    def _(i):
        ct_copy(i).wait_send()

    def settle(q):
        for p in range(nz):
            for k in range(CHUNKS):
                for way in ways(q, p):
                    go_z(way, p, own, k).wait_send()
                    if k >= NEAR_IN:
                        go_z(way, p, side, k).wait_send()
                if k < NEAR_IN or p == q:
                    go_y(p, k).wait_send()
                go_c(p, 0, k).wait_send()
                go_c(p, 1, k).wait_send()
                if k < NEAR_OUT or p == q:
                    share_y(p, k).wait_send()
            for h in range(2):
                for j in range(2):
                    for t in range(2):
                        share(plane(p), h, j, t).wait_send()
            if p != q:
                for at in range(2 * CHUNKS - NEAR_OUT):
                    share_z(AHEAD if p > q else BEHIND, q, p, at).wait_send()

    by_class(settle)


def scratch(n, rows, model, units, pad, hot):
    nz = n // 4
    half, full = jnp.bfloat16, jnp.float32
    dma = pltpu.SemaphoreType.DMA
    piece = rows // CHUNKS
    gathers, reduces = 2 * CHUNKS - NEAR_IN, 2 * CHUNKS - NEAR_OUT
    return [
        pltpu.VMEM((nz, 4, rows, model), half),
        pltpu.VMEM((nz, 2, rows, model), full),
        pltpu.VMEM((nz, 2, rows, model), half),
        pltpu.VMEM((nz, 2, rows, model), half),
        pltpu.VMEM((nz, rows, model), half),
        pltpu.VMEM((nz, rows, model), half),
        pltpu.VMEM((nz, reduces * piece, model), half),
        pltpu.VMEM((nz + 1, reduces * piece, model), half),
        pltpu.VMEM((model, units), half),
        pltpu.VMEM((model, units), half),
        pltpu.VMEM((units, model), half),
        pltpu.VMEM((3 * pad, model), half),
        pltpu.VMEM((2 * rows, units), half),
        pltpu.VMEM((2 * rows, pad), half),
        pltpu.VMEM((n, 8, rows), full),
        pltpu.VMEM((n, 8, rows), full),
        pltpu.VMEM((n, rows, 8), full),
        dma((3 + 3 * hot,)), dma, dma((n,)), dma((n,)),
        dma((nz, gathers)), dma((nz, gathers)), dma((nz, gathers)),
        dma((nz, CHUNKS)), dma((nz, CHUNKS)), dma((nz, 2, CHUNKS)), dma((nz, 2, CHUNKS)),
        dma((nz, 2, 2, 2)), dma((nz, 2, 2, 2)),
        dma((nz, CHUNKS)), dma((nz, CHUNKS)),
        dma((nz, reduces)), dma((nz + 1, reduces)),
    ]


def shards(tokens, w_gate, w_up, w_down, hot_gate, hot_up, hot_down, cold_routes, hot_pick, gates):
    n = lax.axis_size("expert")
    micro_count, local_tokens, model = tokens.shape
    rows = micro_count * local_tokens
    hot, units, part = hot_gate.shape[0], w_gate.shape[2], hot_gate.shape[2]
    pad = -(-hot * part // 128) * 128
    need = rows * model * n * 9 + 3 * model * (units + pad) * 2
    if n != 16 or part % 16 or rows % (16 * CHUNKS) or units % 384 or model % 256 or need > ROOM or hot > 7:
        return routed(
            tokens, w_gate, w_up, w_down, hot_gate, hot_up, hot_down, cold_routes, hot_pick, gates
        )
    anyplace = pl.BlockSpec(memory_space=pl.ANY)
    vmem = pl.BlockSpec(memory_space=pltpu.VMEM)
    mixed = pl.pallas_call(
        functools.partial(fused, n, hot, part),
        out_shape=jax.ShapeDtypeStruct((rows, model), jnp.bfloat16),
        in_specs=[anyplace, vmem, vmem, vmem] + [anyplace] * 6,
        out_specs=vmem,
        scratch_shapes=scratch(n, rows, model, units, pad, hot),
        compiler_params=pltpu.CompilerParams(
            collective_id=0, has_side_effects=True, vmem_limit_bytes=64 * 2**20 - 2**17
        ),
    )(
        tokens.reshape(rows, model), jnp.transpose(cold_routes, (2, 0, 1)), hot_pick,
        jnp.swapaxes(gates, 1, 2),
        w_gate[0], w_up[0], w_down[0],
        *(jnp.swapaxes(w, 1, 2) for w in (hot_gate, hot_up, hot_down)),
    )
    return mixed.reshape(tokens.shape)


def solution(mesh):
    in_specs = (
        P(None, ("groups", "expert"), None),
        P("expert", None, None),
        P("expert", None, None),
        P("expert", None, None),
        P(None, None, "expert"),
        P(None, None, "expert"),
        P(None, None, "expert"),
        P(None, ("groups", "expert"), None),
        P(None, ("groups", "expert")),
        P(None, ("groups", "expert"), None),
    )
    out_specs = P(None, ("groups", "expert"), None)
    return jax.shard_map(shards, mesh=mesh, in_specs=in_specs, out_specs=out_specs, check_vma=False)
```

```python
import functools

import jax
import jax.numpy as jnp
from jax import lax
from jax.experimental import pallas as pl
from jax.experimental.pallas import tpu as pltpu
from jax.sharding import PartitionSpec as P

TOP = 8
HOT = 2


def expert_rows(rows_in, weights):
    leading = rows_in.shape[:-1]
    flat_rows = rows_in.reshape(-1, rows_in.shape[-1])
    gate = jnp.dot(flat_rows, weights[0], preferred_element_type=jnp.float32)
    upward = jnp.dot(flat_rows, weights[1], preferred_element_type=jnp.float32)
    hidden = (jax.nn.silu(gate) * upward).astype(jnp.bfloat16)
    result = jnp.dot(hidden, weights[2], preferred_element_type=jnp.float32).astype(jnp.bfloat16)
    return result.reshape(leading + (result.shape[-1],))


def slot_table(routes_block, axis_width, capacity):
    expert = routes_block.reshape(-1)
    total_count = expert.shape[0]
    onehot = (expert[:, None] == jnp.arange(axis_width, dtype=jnp.int32)[None, :]).astype(jnp.int32)
    before = jnp.cumsum(onehot, axis=0) - onehot
    slot_rank = jnp.sum(before * onehot, axis=1)
    slot_place = expert * capacity + slot_rank
    target = jnp.arange(axis_width * capacity, dtype=jnp.int32)
    matched = slot_place[None, :] == target[:, None]
    filled = jnp.any(matched, axis=1)
    source = jnp.sum(
        jnp.where(matched, jnp.arange(total_count, dtype=jnp.int32)[None, :], 0), axis=1
    )
    return (slot_place, source, filled)


def routed(tokens, w_gate, w_up, w_down, hot_gate, hot_up, hot_down, cold_routes, hot_pick, gates):
    axis_width = lax.axis_size("expert")
    micro_count, local_tokens, model_width = tokens.shape
    picks = TOP - 1
    capacity = local_tokens * picks * 3 // (2 * axis_width) + 1
    own_weights = (w_gate[0], w_up[0], w_down[0])
    outbound = []
    tables = []
    for micro in range(micro_count):
        slot_place, source, filled = slot_table(cold_routes[micro], axis_width, capacity)
        rows_out = tokens[micro][source // picks]
        rows_out = jnp.where(filled[:, None], rows_out, jnp.zeros_like(rows_out))
        outbound.append(rows_out.reshape(axis_width, capacity, model_width))
        tables.append(slot_place)
    joined = jnp.concatenate(outbound, axis=1)
    back_all = lax.all_to_all(
        expert_rows(
            lax.all_to_all(joined, "expert", split_axis=0, concat_axis=0, tiled=True), own_weights
        ),
        "expert",
        split_axis=0,
        concat_axis=0,
        tiled=True,
    )
    returned = [
        back_all[:, micro * capacity : (micro + 1) * capacity] for micro in range(micro_count)
    ]
    cold_parts = []
    for micro in range(micro_count):
        picked = returned[micro].reshape(axis_width * capacity, model_width)[tables[micro]]
        picked = picked.reshape(local_tokens, picks, model_width).astype(jnp.float32)
        cold_parts.append(jnp.sum(picked * gates[micro, :, 1:, None], axis=1))
    cold_total = jnp.stack(cold_parts)
    all_rows = micro_count * local_tokens
    flat = tokens.reshape(all_rows, model_width)
    order = jnp.argsort(hot_pick.reshape(all_rows), stable=True)
    share = all_rows // HOT
    grouped = flat[order].reshape(HOT, share, model_width)
    gate = jnp.einsum(
        "hsd,hdf->hsf",
        grouped,
        lax.all_gather(hot_gate, "expert", axis=2, tiled=True),
        preferred_element_type=jnp.float32,
    )
    upward = jnp.einsum(
        "hsd,hdf->hsf",
        grouped,
        lax.all_gather(hot_up, "expert", axis=2, tiled=True),
        preferred_element_type=jnp.float32,
    )
    hidden = (jax.nn.silu(gate) * upward).astype(jnp.bfloat16)
    hot_sum = jnp.einsum(
        "hsf,hdf->hsd",
        hidden,
        lax.all_gather(hot_down, "expert", axis=2, tiled=True),
        preferred_element_type=jnp.float32,
    )
    sorted_out = hot_sum.astype(jnp.bfloat16).reshape(all_rows, model_width)
    inverse = jnp.argsort(order)
    hot_out = sorted_out[inverse].astype(jnp.float32) * gates[:, :, 0].reshape(all_rows)[:, None]
    total = hot_out.reshape(micro_count, local_tokens, model_width) + cold_total
    return total.astype(jnp.bfloat16)


(
    CROSS_FIRST, SEND_Z, SEND_Y, SEND_CORE, PASS_Z, PASS_CORE, RELAY_OWN, RELAY_SIDE,
    RELAY_CORE, CROSS, REDUCE_SIDE, REDUCE_FAR, REDUCE_NEAR, FINISH_SIDE, FINISH_OWN, STEP,
) = range(16)
OWN, SIDE, FROM_Y, CORE_OWN, CORE_SIDE, SHARE_OWN, SHARE_SIDE, SUM_Y, SUM_Z = range(9)
AHEAD, BEHIND = range(2)
CHUNKS = 8
NEAR_IN = 7
NEAR_OUT = 5
HIGH = (4, 6, 7, 5)
LOW = (2, 1, 3, 0)
STEPS = 6
TABLE_WITH = 4
UNITS = (
    ((1, 0), (0, 0), (2, 0), (3, 0), (1, 1), (3, 1), (2, 1), (0, 1)),
    ((1, 1), (0, 0), (3, 0), (2, 0), (3, 1), (0, 1), (2, 1), (1, 0)),
)
OUTER = (
    (SEND_Y, 1), (SEND_CORE,), (SEND_Z, 4, AHEAD), (CROSS_FIRST,), (SEND_Z, 7, AHEAD),
    (SEND_Y, 2), (SEND_Z, 6, AHEAD), (SEND_Y, 3), (PASS_CORE, 1), (SEND_Z, 5, AHEAD),
    (RELAY_OWN, 1, 6), (PASS_Z, 7), (PASS_CORE, 7), (RELAY_OWN, 1, 4), (PASS_CORE, 2),
    (SEND_Z, 2, AHEAD), (RELAY_OWN, 1, 5), (SEND_Z, 3, AHEAD), (SEND_Y, 4), (PASS_CORE, 3),
    (SEND_Y, 6), (RELAY_OWN, 2, 4), (RELAY_CORE, 1, 6), (RELAY_SIDE, 1, 7), (RELAY_CORE, 1, 4),
    (SEND_Z, 1, AHEAD), (RELAY_OWN, 1, 7), (SEND_Z, 0, AHEAD), (RELAY_CORE, 1, 5),
    (RELAY_OWN, 1, 1), (SEND_Y, 5), (STEP, 0, 0), (PASS_CORE, 4), (RELAY_OWN, 2, 6), (STEP, 0, 1),
    (STEP, 0, 2), (STEP, 0, 3), (STEP, 0, 4), (RELAY_OWN, 3, 4), (STEP, 0, 5), (PASS_CORE, 6),
    (RELAY_OWN, 2, 5), (RELAY_CORE, 1, 1), (RELAY_OWN, 1, 3), (RELAY_CORE, 2, 4),
    (REDUCE_FAR, 1, 7), (REDUCE_FAR, 1, 5), (REDUCE_FAR, 1, 6), (REDUCE_SIDE, 1, 5),
    (REDUCE_SIDE, 1, 6), (REDUCE_SIDE, 1, 7), (PASS_CORE, 5), (CROSS, 1, 4), (RELAY_OWN, 2, 7),
    (STEP, 1, 0), (RELAY_CORE, 2, 6), (RELAY_OWN, 1, 0), (STEP, 1, 1), (RELAY_OWN, 2, 0),
    (RELAY_CORE, 3, 4), (STEP, 1, 2), (STEP, 1, 3), (RELAY_OWN, 1, 2), (RELAY_CORE, 2, 5),
    (STEP, 1, 4), (STEP, 1, 5), (RELAY_SIDE, 2, 7), (RELAY_CORE, 1, 3), (REDUCE_NEAR, 1, 4),
    (CROSS, 0, 4), (RELAY_OWN, 3, 6), (STEP, 2, 0), (STEP, 2, 1), (RELAY_OWN, 3, 5), (STEP, 2, 2),
    (RELAY_SIDE, 3, 7), (STEP, 2, 3), (STEP, 2, 4), (STEP, 2, 5), (RELAY_CORE, 1, 2),
    (RELAY_CORE, 2, 0), (RELAY_OWN, 3, 3), (RELAY_CORE, 1, 0), (SEND_Y, 0), (RELAY_OWN, 3, 0),
    (REDUCE_FAR, 2, 7), (REDUCE_FAR, 2, 5), (REDUCE_FAR, 2, 6), (REDUCE_SIDE, 2, 5),
    (REDUCE_SIDE, 2, 7), (REDUCE_SIDE, 2, 6), (CROSS, 2, 4), (RELAY_CORE, 3, 6),
    (RELAY_OWN, 3, 7), (RELAY_CORE, 3, 5), (RELAY_OWN, 3, 1), (STEP, 3, 0), (RELAY_CORE, 3, 3),
    (RELAY_OWN, 3, 2), (STEP, 3, 1), (RELAY_OWN, 2, 3), (PASS_CORE, 0), (STEP, 3, 2),
    (STEP, 3, 3), (RELAY_CORE, 3, 0), (STEP, 3, 4), (STEP, 3, 5), (REDUCE_NEAR, 2, 4),
    (RELAY_OWN, 2, 1), (RELAY_OWN, 2, 2), (STEP, 4, 0), (REDUCE_FAR, 3, 6), (REDUCE_FAR, 3, 7),
    (STEP, 4, 1), (REDUCE_SIDE, 3, 7), (REDUCE_SIDE, 3, 6), (RELAY_CORE, 3, 1),
    (REDUCE_SIDE, 3, 5), (CROSS, 3, 4), (STEP, 4, 2), (RELAY_CORE, 3, 2), (STEP, 4, 3),
    (STEP, 4, 4), (RELAY_CORE, 2, 3), (STEP, 4, 5), (STEP, 5, 0), (STEP, 5, 1), (CROSS, 1, 3),
    (CROSS, 1, 2), (CROSS, 1, 1), (STEP, 5, 2), (STEP, 5, 3), (REDUCE_NEAR, 3, 4), (STEP, 5, 4),
    (STEP, 5, 5), (RELAY_CORE, 2, 2), (REDUCE_FAR, 3, 5), (REDUCE_NEAR, 1, 3), (CROSS, 1, 0),
    (RELAY_CORE, 2, 1), (CROSS, 3, 3), (CROSS, 3, 0), (CROSS, 3, 2), (CROSS, 3, 1),
    (REDUCE_NEAR, 1, 2), (STEP, 6, 0), (STEP, 6, 1), (REDUCE_NEAR, 1, 1), (STEP, 6, 2),
    (REDUCE_NEAR, 1, 0), (STEP, 6, 3), (STEP, 6, 4), (STEP, 6, 5), (STEP, 7, 0),
    (FINISH_SIDE, 0, 6), (REDUCE_NEAR, 3, 0), (STEP, 7, 1), (CROSS, 2, 3), (CROSS, 2, 2),
    (STEP, 7, 2), (REDUCE_NEAR, 3, 2), (FINISH_OWN, 0, 4), (STEP, 7, 3), (STEP, 7, 4),
    (REDUCE_NEAR, 3, 1), (STEP, 7, 5), (CROSS, 2, 0), (CROSS, 2, 1), (REDUCE_NEAR, 3, 3),
    (FINISH_SIDE, 0, 7), (CROSS, 0, 0), (CROSS, 0, 3), (CROSS, 0, 2), (CROSS, 0, 1),
    (REDUCE_NEAR, 2, 3), (REDUCE_NEAR, 2, 2), (REDUCE_NEAR, 2, 0), (FINISH_SIDE, 0, 5),
    (REDUCE_NEAR, 2, 1), (FINISH_OWN, 0, 6), (FINISH_OWN, 0, 7), (FINISH_OWN, 0, 0),
    (FINISH_OWN, 0, 2), (FINISH_OWN, 0, 3), (FINISH_OWN, 0, 1), (FINISH_OWN, 0, 5),
)
INNER = (
    (SEND_CORE,), (SEND_Z, 6, BEHIND), (SEND_Z, 4, AHEAD), (SEND_Z, 4, BEHIND),
    (SEND_Z, 7, AHEAD), (CROSS_FIRST,), (SEND_Y, 1), (SEND_Z, 6, AHEAD), (SEND_Y, 3),
    (SEND_Z, 5, BEHIND), (SEND_Z, 5, AHEAD), (RELAY_OWN, 0, 4), (RELAY_OWN, 2, 4), (PASS_CORE, 7),
    (SEND_Z, 0, AHEAD), (PASS_Z, 7), (SEND_Z, 7, BEHIND), (SEND_Y, 0), (PASS_CORE, 1),
    (SEND_Z, 1, BEHIND), (RELAY_OWN, 2, 6), (PASS_CORE, 3), (RELAY_OWN, 0, 6), (RELAY_OWN, 0, 5),
    (SEND_Y, 4), (RELAY_CORE, 0, 4), (RELAY_SIDE, 0, 7), (SEND_Y, 2), (RELAY_OWN, 3, 4),
    (RELAY_CORE, 2, 4), (RELAY_OWN, 2, 5), (SEND_Z, 3, BEHIND), (RELAY_OWN, 2, 7),
    (SEND_Z, 0, BEHIND), (RELAY_OWN, 2, 0), (SEND_Z, 2, BEHIND), (PASS_CORE, 0),
    (RELAY_OWN, 0, 3), (SEND_Z, 2, AHEAD), (RELAY_CORE, 2, 6), (RELAY_SIDE, 2, 7),
    (RELAY_OWN, 3, 6), (RELAY_CORE, 0, 6), (RELAY_OWN, 0, 1), (RELAY_OWN, 3, 5),
    (RELAY_OWN, 0, 0), (RELAY_CORE, 0, 5), (RELAY_SIDE, 3, 7), (PASS_CORE, 4), (RELAY_OWN, 0, 2),
    (PASS_CORE, 2), (RELAY_OWN, 3, 3), (STEP, 0, 0), (RELAY_OWN, 0, 7), (STEP, 0, 1),
    (STEP, 0, 2), (STEP, 0, 3), (RELAY_OWN, 3, 0), (RELAY_CORE, 2, 0), (STEP, 0, 4), (STEP, 0, 5),
    (SEND_Z, 3, AHEAD), (RELAY_CORE, 0, 3), (SEND_Z, 1, AHEAD), (STEP, 1, 0), (STEP, 1, 1),
    (CROSS, 1, 3), (CROSS, 1, 0), (RELAY_OWN, 3, 7), (SEND_Y, 6), (CROSS, 1, 1),
    (RELAY_CORE, 3, 6), (STEP, 1, 2), (RELAY_OWN, 3, 1), (STEP, 1, 3), (STEP, 1, 4),
    (RELAY_CORE, 3, 5), (RELAY_OWN, 3, 2), (STEP, 1, 5), (RELAY_OWN, 2, 3), (RELAY_CORE, 3, 4),
    (CROSS, 1, 2), (RELAY_CORE, 2, 5), (RELAY_OWN, 2, 2), (RELAY_OWN, 2, 1), (RELAY_CORE, 0, 1),
    (SEND_Y, 5), (RELAY_CORE, 0, 0), (CROSS, 0, 4), (STEP, 2, 0), (STEP, 2, 1),
    (RELAY_CORE, 3, 3), (STEP, 2, 2), (STEP, 2, 3), (RELAY_CORE, 3, 0), (STEP, 2, 4),
    (STEP, 2, 5), (STEP, 3, 0), (STEP, 3, 1), (STEP, 3, 2), (STEP, 3, 3), (STEP, 3, 4),
    (STEP, 3, 5), (RELAY_CORE, 0, 2), (PASS_CORE, 6), (CROSS, 3, 4), (REDUCE_FAR, 2, 7),
    (REDUCE_FAR, 2, 6), (REDUCE_FAR, 2, 5), (RELAY_CORE, 3, 1), (CROSS, 2, 4),
    (REDUCE_SIDE, 2, 5), (REDUCE_SIDE, 2, 7), (RELAY_CORE, 3, 2), (REDUCE_SIDE, 2, 6),
    (STEP, 4, 0), (STEP, 4, 1), (STEP, 4, 2), (STEP, 4, 3), (STEP, 4, 4), (REDUCE_FAR, 3, 7),
    (RELAY_CORE, 2, 2), (STEP, 4, 5), (STEP, 5, 0), (STEP, 5, 1), (CROSS, 3, 2),
    (REDUCE_SIDE, 3, 6), (STEP, 5, 2), (STEP, 5, 3), (REDUCE_SIDE, 3, 5), (STEP, 5, 4),
    (STEP, 5, 5), (REDUCE_FAR, 0, 7), (REDUCE_NEAR, 3, 4), (RELAY_CORE, 2, 1), (REDUCE_FAR, 3, 6),
    (CROSS, 3, 3), (CROSS, 3, 0), (RELAY_CORE, 2, 3), (PASS_CORE, 5), (REDUCE_SIDE, 3, 7),
    (CROSS, 3, 1), (REDUCE_SIDE, 0, 6), (REDUCE_NEAR, 2, 4), (REDUCE_FAR, 3, 5), (CROSS, 0, 2),
    (CROSS, 0, 3), (CROSS, 0, 1), (CROSS, 0, 0), (STEP, 6, 0), (STEP, 6, 1), (STEP, 6, 2),
    (REDUCE_NEAR, 0, 4), (STEP, 6, 3), (STEP, 6, 4), (STEP, 6, 5), (STEP, 7, 0),
    (REDUCE_SIDE, 0, 7), (STEP, 7, 1), (CROSS, 2, 3), (CROSS, 2, 0), (STEP, 7, 2),
    (REDUCE_NEAR, 3, 0), (STEP, 7, 3), (REDUCE_FAR, 0, 5), (STEP, 7, 4), (REDUCE_NEAR, 3, 2),
    (STEP, 7, 5), (REDUCE_SIDE, 0, 5), (CROSS, 2, 2), (CROSS, 2, 1), (REDUCE_FAR, 0, 6),
    (REDUCE_NEAR, 3, 1), (FINISH_SIDE, 1, 6), (CROSS, 1, 4), (FINISH_SIDE, 1, 7),
    (FINISH_SIDE, 1, 5), (REDUCE_NEAR, 0, 0), (REDUCE_NEAR, 3, 3), (REDUCE_NEAR, 0, 2),
    (REDUCE_NEAR, 2, 3), (REDUCE_NEAR, 0, 1), (REDUCE_NEAR, 0, 3), (REDUCE_NEAR, 2, 2),
    (REDUCE_NEAR, 2, 0), (FINISH_OWN, 1, 3), (REDUCE_NEAR, 2, 1), (FINISH_OWN, 1, 6),
    (FINISH_OWN, 1, 2), (FINISH_OWN, 1, 4), (FINISH_OWN, 1, 0), (FINISH_OWN, 1, 7),
    (FINISH_OWN, 1, 1), (FINISH_OWN, 1, 5),
)
ROOM = 56 * 2**20


def tile_of(extent, most):
    return most if extent % most == 0 else extent


def needs(q, nz, task):
    name, *at = task
    if name in (CROSS_FIRST, SEND_Z, SEND_Y, SEND_CORE):
        return []
    if name in (PASS_Z, PASS_CORE):
        return [(FROM_Y, q, at[0])]
    p, k = at
    if name == RELAY_OWN:
        return [(OWN, p, k)]
    if name == RELAY_SIDE:
        return [(SIDE, p, k)]
    if name == RELAY_CORE:
        return [(FROM_Y, p, k)]
    h = 0 if k >= CHUNKS // 2 else 1
    own, side = ([(share, p, h, t) for t in range(2)] for share in (SHARE_OWN, SHARE_SIDE))
    if p == q:
        came = [w for w, there in ((AHEAD, q > 0), (BEHIND, q < nz - 1)) if there]
    else:
        came = [w for w, there in ((AHEAD, p > q > 0), (BEHIND, p < q < nz - 1)) if there]
    far = [(SUM_Z, p, CHUNKS + k - NEAR_OUT, w) for w in came]
    mine = [(SUM_Z, p, k, w) for w in came]
    cross = [(SUM_Y, p, k)]
    return {
        CROSS: side, REDUCE_SIDE: side + far, FINISH_SIDE: side + far,
        REDUCE_FAR: own + mine, REDUCE_NEAR: own + cross + mine, FINISH_OWN: own + cross + mine,
    }[name]


def hooks(q, nz, tasks):
    at, waited = (-1, STEPS - 1), set()
    plan = {at: []}

    def fresh(keys):
        news = [key for key in keys if key not in waited]
        waited.update(news)
        return news

    for task in tasks:
        if task[0] != STEP:
            plan[at].append((fresh(needs(q, nz, task)), task))
            continue
        if task[2] == 0:
            p, h = UNITS[q][task[1]]
            half = range(CHUNKS // 2, CHUNKS) if h == 0 else range(CHUNKS // 2)
            half = {*half, TABLE_WITH}
            keys = [(core, p, k) for core in (CORE_OWN, CORE_SIDE) for k in half]
            keys += [(FROM_Y, p, k) for k in half if p == q or k < NEAR_IN]
            if p != q:
                keys += [(OWN, p, k) for k in half]
                keys += [(SIDE, p, k) for k in half if k >= NEAR_IN]
            plan[at].append((fresh(keys), None))
        at = (task[1], task[2])
        plan[at] = []
    return plan


def fused(
    n, hot, part, tok, routes, pick, gts, wg_in, wu_in, wd_in, hg_in, hu_in, hd_in, out,
    xs, keep, sc, rc, sy, ry, sz, rz, wg, wu, wd, wh, hid, hhid, table, gw,
    wsem, tsem, tu_s, td_s, tz_r, ty_s, ty_r, tc_s, tc_r, up_s, down_s, z_r, y_s, y_r, c_s, c_r,
    rc_s, rc_r, ry_s, ry_r, rz_s, rz_r,
):
    nz = n // 4
    rows, model = tok.shape
    units = wg.shape[1]
    pad = hhid.shape[1]
    piece = rows // CHUNKS
    half = rows // 2
    wide = units // 3
    band = model // 2
    tile = tile_of(band, 512)
    me = lax.axis_index("expert")
    c = lax.rem(me, 2)
    y = lax.rem(lax.div(me, 2), 2)
    z = lax.div(me, 4)
    own = y * 2 + c
    side = (1 - y) * 2 + c
    peer_y = z * 4 + side
    peer_c = z * 4 + y * 2 + (1 - c)
    outer = (z == 0) | (z == nz - 1)
    low = z * 2 < nz

    def plane(p):
        return jnp.where(low, p, nz - 1 - p)

    ahead = me + jnp.where(low, 4, -4)
    behind = me - jnp.where(low, 4, -4)

    def remote(src, dst, send, recv, device):
        return pltpu.make_async_remote_copy(
            src_ref=src, dst_ref=dst, send_sem=send, recv_sem=recv,
            device_id={"expert": device}, device_id_type=pl.DeviceIdType.MESH,
        )

    def span(k):
        return pl.ds(k * piece, piece)

    loads = [
        pltpu.make_async_copy(src, dst, wsem.at[i])
        for i, (src, dst) in enumerate((
            *(
                (src.at[h], wh.at[pl.ds(t * pad + h * part, part)])
                for t, src in enumerate((hg_in, hu_in, hd_in)) for h in range(hot)
            ),
            (wg_in, wg), (wu_in, wu), (wd_in, wd),
        ))
    ]
    first = pltpu.make_async_copy(tok, xs.at[z, own], tsem)
    first.start()
    barrier = pltpu.get_barrier_semaphore()

    def greet(device):
        pl.semaphore_signal(
            barrier, inc=1, device_id={"expert": device},
            device_id_type=pl.DeviceIdType.MESH,
        )

    greet(peer_c)
    greet(peer_y)
    greet(ahead)

    @pl.when(jnp.logical_not(outer))
    def _():
        greet(behind)

    table[me] = jnp.zeros(table.shape[1:], jnp.float32)
    micros = gts.shape[0]

    def joined(parts):
        return jnp.concatenate(parts, axis=1)

    warm_row = joined([gts[m, 0:1, :] for m in range(micros)])
    chosen = joined([pick[m : m + 1, :] for m in range(micros)])
    named = [
        (
            joined([routes[k, m : m + 1, :] for m in range(micros)]),
            joined([gts[m, k + 1 : k + 2, :] for m in range(micros)]),
        )
        for k in range(routes.shape[0])
    ]

    def row(e):
        return sum(jnp.where(route == e, weight, 0.0) for route, weight in named)

    for e in range(n):
        table[me, e : e + 1, :] = row(e)
    for h in range(hot):
        table[me, n + h : n + h + 1, :] = jnp.where(chosen == h, warm_row, 0.0)

    first.wait()
    for load in loads:
        load.start()
    pl.semaphore_wait(barrier, jnp.where(outer, 3, 4))

    def table_z(way, p):
        ref = table.at[plane(p) * 4 + own]
        send = tu_s if way == AHEAD else td_s
        return remote(
            ref, ref, send.at[plane(p)], tz_r.at[plane(p)], ahead if way == AHEAD else behind
        )

    def table_y(p):
        ref = table.at[plane(p) * 4 + own]
        return remote(ref, ref, ty_s.at[plane(p)], ty_r.at[plane(p)], peer_y)

    def table_c(p, which):
        ref = table.at[plane(p) * 4 + (own, side)[which]]
        return remote(ref, ref, tc_s.at[plane(p), which], tc_r.at[plane(p), which], peer_c)

    def go_z(way, p, slot, k):
        at = k if slot is own else CHUNKS + k - NEAR_IN
        ref = xs.at[plane(p), slot, span(k)]
        send = up_s if way == AHEAD else down_s
        return remote(
            ref, ref, send.at[plane(p), at], z_r.at[plane(p), at],
            ahead if way == AHEAD else behind,
        )

    def go_y(p, k):
        ref = xs.at[plane(p), own, span(k)]
        return remote(ref, ref, y_s.at[plane(p), k], y_r.at[plane(p), k], peer_y)

    def go_c(p, which, k):
        ref = xs.at[plane(p), (own, side)[which], span(k)]
        return remote(
            ref, ref, c_s.at[plane(p), which, k], c_r.at[plane(p), which, k], peer_c
        )

    def share(at, h, j, t):
        lines = pl.ds(pl.multiple_of((1 - h) * half, half), half)
        cols = pl.ds(t * band, band)
        return remote(
            sc.at[at, j, lines, cols], rc.at[at, j, lines, cols],
            rc_s.at[at, h, j, t], rc_r.at[at, h, j, t], peer_c,
        )

    def share_y(p, k):
        at = plane(p)
        return remote(
            sy.at[at, span(k)], ry.at[at, span(k)], ry_s.at[at, k], ry_r.at[at, k], peer_y
        )

    def landing(way, p, last):
        if not last:
            return plane(p)
        return jnp.where(low == (way == AHEAD), plane(p), nz)

    def share_z(way, q, p, at):
        slot = landing(way, p, p == (q + 1 if way == AHEAD else q - 1))
        return remote(
            sz.at[plane(p), span(at)], rz.at[slot, span(at)],
            rz_s.at[plane(p), at], rz_r.at[slot, at],
            ahead if way == AHEAD else behind,
        )

    def await_event(q, key):
        name, p, k, *rest = key
        tabled = k == TABLE_WITH
        if name == OWN:
            if tabled:
                table_z(AHEAD, p).wait_recv()
            go_z(AHEAD, p, own, k).wait_recv()
        elif name == SIDE:
            go_z(AHEAD, p, side, k).wait_recv()
        elif name == FROM_Y:
            if tabled:
                table_y(p).wait_recv()
            ref = xs.at[plane(p), side, span(k)]
            remote(ref, ref, y_s.at[plane(p), k], y_r.at[plane(p), k], peer_y).wait_recv()
        elif name in (CORE_OWN, CORE_SIDE):
            if tabled:
                table_c(p, int(name == CORE_SIDE)).wait_recv()
            go_c(p, int(name == CORE_SIDE), k).wait_recv()
        elif name in (SHARE_OWN, SHARE_SIDE):
            share(plane(p), k, y if name == SHARE_OWN else 1 - y, rest[0]).wait_recv()
        elif name == SUM_Y:
            share_y(p, k).wait_recv()
        else:
            slot = landing(rest[0], p, p == q)
            ref = rz.at[slot, span(k)]
            remote(ref, ref, rz_s.at[0, k], rz_r.at[slot, k], me).wait_recv()

    def ways(q, p):
        return (AHEAD,) * (p <= q and q + 1 < nz) + (BEHIND,) * (p >= q and q > 0)

    def add_up(dst, lines, terms):
        @pl.loop(0, model // tile)
        def _(t):
            cols = pl.ds(pl.multiple_of(t * tile, tile), tile)
            total = None
            for term in terms:
                value = term(cols).astype(jnp.float32)
                total = value if total is None else total + value
            dst[lines, cols] = total.astype(jnp.bfloat16)

    def act(q, task):
        name, *at = task
        if name == CROSS_FIRST:
            for k in HIGH + LOW:
                if k >= NEAR_IN:
                    go_y(q, k).start()
        elif name == SEND_Z:
            if at[0] == TABLE_WITH:
                table_z(at[1], q).start()
            go_z(at[1], q, own, at[0]).start()
        elif name == SEND_CORE:
            table_c(q, 0).start()
            for k in range(CHUNKS):
                go_c(q, 0, k).start()
        elif name == PASS_Z:
            for way in ways(q, q):
                go_z(way, q, side, at[0]).start()
        elif name == SEND_Y:
            if at[0] == TABLE_WITH:
                table_y(q).start()
            go_y(q, at[0]).start()
        elif name == PASS_CORE:
            if at[0] == TABLE_WITH:
                table_c(q, 1).start()
            go_c(q, 1, at[0]).start()
        elif name == RELAY_OWN:
            p, k = at
            if k == TABLE_WITH:
                for way in ways(q, p):
                    table_z(way, p).start()
                table_y(p).start()
                table_c(p, 0).start()
            for way in ways(q, p):
                go_z(way, p, own, k).start()
            if k < NEAR_IN:
                go_y(p, k).start()
            go_c(p, 0, k).start()
        elif name == RELAY_SIDE:
            p, k = at
            for way in ways(q, p):
                go_z(way, p, side, k).start()
            go_c(p, 1, k).start()
        elif name == RELAY_CORE:
            if at[1] == TABLE_WITH:
                table_c(at[0], 1).start()
            go_c(at[0], 1, at[1]).start()
        else:
            p, k = at
            j = 1 - y if name in (CROSS, REDUCE_SIDE, FINISH_SIDE) else y
            here = plane(p)
            terms = [
                lambda cols: keep[here, j, span(k), cols],
                lambda cols: rc[here, j, span(k), cols],
            ]
            for key in needs(q, nz, task):
                if key[0] == SUM_Y:
                    terms.append(lambda cols: ry[here, span(k), cols])
                if key[0] == SUM_Z:
                    slot, line = landing(key[3], p, p == q), span(key[2])
                    terms.append(lambda cols, slot=slot, line=line: rz[slot, line, cols])
            if name in (CROSS, FINISH_SIDE):
                add_up(sy.at[here], span(k), terms)
                share_y(p, k).start()
            elif name == FINISH_OWN:
                add_up(out, span(k), terms)
            else:
                line = CHUNKS + k - NEAR_OUT if name == REDUCE_SIDE else k
                add_up(sz.at[here], span(line), terms)
                share_z(AHEAD if p > q else BEHIND, q, p, line).start()

    plans = [hooks(q, nz, tasks) for q, tasks in enumerate((OUTER, INNER))]

    def perform(q, steps):
        for keys, task in steps:
            for key in keys:
                await_event(q, key)
            if task is not None:
                act(q, task)

    def by_class(emit):
        @pl.when(outer)
        def _():
            emit(0)

        @pl.when(jnp.logical_not(outer))
        def _():
            emit(1)

    count = len(UNITS[0])

    def hook(u, step):
        def emit(q):
            for j in range(count):
                if (j, step) != (count - 1, STEPS - 1) and plans[q].get((j, step)):
                    @pl.when(u == j)
                    def _():
                        perform(q, plans[q][j, step])

        by_class(emit)

    def picked(u, field):
        found = [
            functools.reduce(
                lambda rest, j: jnp.where(u == j, UNITS[q][j][field], rest),
                range(1, count), jnp.int32(UNITS[q][0][field]),
            )
            for q in range(2)
        ]
        return jnp.where(outer, *found)

    def take_weights():
        if pad > hot * part:
            for t in range(3):
                blank = wh.at[pl.ds(t * pad + hot * part, pad - hot * part)]
                blank[...] = jnp.zeros_like(blank)

        for load in loads:
            load.wait()

    def start(q):
        for keys, task in plans[q][-1, STEPS - 1]:
            if task is None:
                take_weights()
            perform(q, [(keys, task)])

    by_class(start)

    @pl.loop(0, count)
    def _(u):
        here = plane(picked(u, 0))
        h = picked(u, 1)
        lines = pl.ds(pl.multiple_of((1 - h) * half, half), half)

        def block():
            return xs[here, :, lines, :].reshape(4 * half, model)

        for j in range(4):
            given = [table[here * 4 + j, pl.ds(me, 1), :]]
            given += [table[here * 4 + j, n + i : n + i + 1, :] for i in range(hot)]
            given.append(jnp.zeros((8 - len(given), rows), jnp.float32))
            gw[j] = jnp.transpose(jnp.concatenate(given, axis=0))

        def columns(which):
            return jnp.concatenate(
                [gw[j, lines, which : which + 1] for j in range(4)], axis=0
            )

        for i in range(3):
            cols = pl.ds(i * wide, wide)
            v = block()
            g = jnp.dot(v, wg[:, cols], preferred_element_type=jnp.float32)
            up = jnp.dot(v, wu[:, cols], preferred_element_type=jnp.float32)
            hid[:, cols] = (g / (1.0 + jnp.exp(-g)) * up).astype(jnp.bfloat16)
            hook(u, i)

        gu = lax.dot_general(
            block(), wh[: 2 * pad, :], (((1,), (1,)), ((), ())),
            preferred_element_type=jnp.float32,
        )
        g, up = gu[:, :pad], gu[:, pad:]
        lane = lax.broadcasted_iota(jnp.int32, (4 * half, pad), 1)
        warm = jnp.zeros((4 * half, pad), jnp.float32)
        for i in range(hot):
            warm = jnp.where((lane >= i * part) & (lane < (i + 1) * part), columns(1 + i), warm)
        hhid[...] = (g / (1.0 + jnp.exp(-g)) * up * warm).astype(jnp.bfloat16)
        hook(u, 3)

        cold = columns(0)
        for t in range(2):
            for i in range(band // tile):
                cols = pl.ds(t * band + i * tile, tile)
                r = jnp.dot(hid[...], wd[:, cols], preferred_element_type=jnp.float32)
                r = r.astype(jnp.bfloat16).astype(jnp.float32) * cold
                r = r + jnp.dot(
                    hhid[...], wh[2 * pad :, cols], preferred_element_type=jnp.float32
                )
                for j in range(2):
                    even = r[2 * j * half : (2 * j + 1) * half]
                    odd = r[(2 * j + 1) * half : (2 * j + 2) * half]
                    keep[here, j, lines, cols] = jnp.where(c == 0, even, odd)
                    sc[here, j, lines, cols] = jnp.where(c == 0, odd, even).astype(jnp.bfloat16)
            share(here, h, 1 - y, t).start()
            share(here, h, y, t).start()
            hook(u, 4 + t)

    by_class(lambda q: perform(q, plans[q][count - 1, STEPS - 1]))

    def settle(q):
        for p in range(nz):
            for way in ways(q, p):
                table_z(way, p).wait_send()
            table_y(p).wait_send()
            table_c(p, 0).wait_send()
            table_c(p, 1).wait_send()
            for k in range(CHUNKS):
                for way in ways(q, p):
                    go_z(way, p, own, k).wait_send()
                    if k >= NEAR_IN:
                        go_z(way, p, side, k).wait_send()
                if k < NEAR_IN or p == q:
                    go_y(p, k).wait_send()
                go_c(p, 0, k).wait_send()
                go_c(p, 1, k).wait_send()
                if k < NEAR_OUT or p == q:
                    share_y(p, k).wait_send()
            for h in range(2):
                for j in range(2):
                    for t in range(2):
                        share(plane(p), h, j, t).wait_send()
            if p != q:
                for at in range(2 * CHUNKS - NEAR_OUT):
                    share_z(AHEAD if p > q else BEHIND, q, p, at).wait_send()

    by_class(settle)


def scratch(n, rows, model, units, pad, hot):
    nz = n // 4
    half, full = jnp.bfloat16, jnp.float32
    dma = pltpu.SemaphoreType.DMA
    piece = rows // CHUNKS
    gathers, reduces = 2 * CHUNKS - NEAR_IN, 2 * CHUNKS - NEAR_OUT
    return [
        pltpu.VMEM((nz, 4, rows, model), half),
        pltpu.VMEM((nz, 2, rows, model), full),
        pltpu.VMEM((nz, 2, rows, model), half),
        pltpu.VMEM((nz, 2, rows, model), half),
        pltpu.VMEM((nz, rows, model), half),
        pltpu.VMEM((nz, rows, model), half),
        pltpu.VMEM((nz, reduces * piece, model), half),
        pltpu.VMEM((nz + 1, reduces * piece, model), half),
        pltpu.VMEM((model, units), half),
        pltpu.VMEM((model, units), half),
        pltpu.VMEM((units, model), half),
        pltpu.VMEM((3 * pad, model), half),
        pltpu.VMEM((2 * rows, units), half),
        pltpu.VMEM((2 * rows, pad), half),
        pltpu.VMEM((n, -(-(n + hot) // 8) * 8, rows), full),
        pltpu.VMEM((4, rows, 8), full),
        dma((3 + 3 * hot,)), dma, dma((nz,)), dma((nz,)), dma((nz,)),
        dma((nz,)), dma((nz,)), dma((nz, 2)), dma((nz, 2)),
        dma((nz, gathers)), dma((nz, gathers)), dma((nz, gathers)),
        dma((nz, CHUNKS)), dma((nz, CHUNKS)), dma((nz, 2, CHUNKS)), dma((nz, 2, CHUNKS)),
        dma((nz, 2, 2, 2)), dma((nz, 2, 2, 2)),
        dma((nz, CHUNKS)), dma((nz, CHUNKS)),
        dma((nz, reduces)), dma((nz + 1, reduces)),
    ]


def shards(tokens, w_gate, w_up, w_down, hot_gate, hot_up, hot_down, cold_routes, hot_pick, gates):
    n = lax.axis_size("expert")
    micro_count, local_tokens, model = tokens.shape
    rows = micro_count * local_tokens
    hot, units, part = hot_gate.shape[0], w_gate.shape[2], hot_gate.shape[2]
    pad = -(-hot * part // 128) * 128
    need = rows * model * n * 9 + 3 * model * (units + pad) * 2
    if n != 16 or part % 16 or rows % (16 * CHUNKS) or units % 384 or model % 256 or need > ROOM or hot > 7:
        return routed(
            tokens, w_gate, w_up, w_down, hot_gate, hot_up, hot_down, cold_routes, hot_pick, gates
        )
    anyplace = pl.BlockSpec(memory_space=pl.ANY)
    vmem = pl.BlockSpec(memory_space=pltpu.VMEM)
    mixed = pl.pallas_call(
        functools.partial(fused, n, hot, part),
        out_shape=jax.ShapeDtypeStruct((rows, model), jnp.bfloat16),
        in_specs=[anyplace, vmem, vmem, vmem] + [anyplace] * 6,
        out_specs=vmem,
        scratch_shapes=scratch(n, rows, model, units, pad, hot),
        compiler_params=pltpu.CompilerParams(
            collective_id=0, has_side_effects=True, vmem_limit_bytes=64 * 2**20 - 2**17
        ),
    )(
        tokens.reshape(rows, model), jnp.transpose(cold_routes, (2, 0, 1)), hot_pick,
        jnp.swapaxes(gates, 1, 2),
        w_gate[0], w_up[0], w_down[0],
        *(jnp.swapaxes(w, 1, 2) for w in (hot_gate, hot_up, hot_down)),
    )
    return mixed.reshape(tokens.shape)


def solution(mesh):
    in_specs = (
        P(None, ("groups", "expert"), None),
        P("expert", None, None),
        P("expert", None, None),
        P("expert", None, None),
        P(None, None, "expert"),
        P(None, None, "expert"),
        P(None, None, "expert"),
        P(None, ("groups", "expert"), None),
        P(None, ("groups", "expert")),
        P(None, ("groups", "expert"), None),
    )
    out_specs = P(None, ("groups", "expert"), None)
    return jax.shard_map(shards, mesh=mesh, in_specs=in_specs, out_specs=out_specs, check_vma=False)
```

```python
import functools

import jax
import jax.numpy as jnp
from jax import lax
from jax.experimental import pallas as pl
from jax.experimental.pallas import tpu as pltpu
from jax.sharding import PartitionSpec as P

TOP = 8
HOT = 2


def expert_rows(rows_in, weights):
    leading = rows_in.shape[:-1]
    flat_rows = rows_in.reshape(-1, rows_in.shape[-1])
    gate = jnp.dot(flat_rows, weights[0], preferred_element_type=jnp.float32)
    upward = jnp.dot(flat_rows, weights[1], preferred_element_type=jnp.float32)
    hidden = (jax.nn.silu(gate) * upward).astype(jnp.bfloat16)
    result = jnp.dot(hidden, weights[2], preferred_element_type=jnp.float32).astype(jnp.bfloat16)
    return result.reshape(leading + (result.shape[-1],))


def slot_table(routes_block, axis_width, capacity):
    expert = routes_block.reshape(-1)
    total_count = expert.shape[0]
    onehot = (expert[:, None] == jnp.arange(axis_width, dtype=jnp.int32)[None, :]).astype(jnp.int32)
    before = jnp.cumsum(onehot, axis=0) - onehot
    slot_rank = jnp.sum(before * onehot, axis=1)
    slot_place = expert * capacity + slot_rank
    target = jnp.arange(axis_width * capacity, dtype=jnp.int32)
    matched = slot_place[None, :] == target[:, None]
    filled = jnp.any(matched, axis=1)
    source = jnp.sum(
        jnp.where(matched, jnp.arange(total_count, dtype=jnp.int32)[None, :], 0), axis=1
    )
    return (slot_place, source, filled)


def routed(tokens, w_gate, w_up, w_down, hot_gate, hot_up, hot_down, cold_routes, hot_pick, gates):
    axis_width = lax.axis_size("expert")
    micro_count, local_tokens, model_width = tokens.shape
    picks = TOP - 1
    capacity = local_tokens * picks * 3 // (2 * axis_width) + 1
    own_weights = (w_gate[0], w_up[0], w_down[0])
    outbound = []
    tables = []
    for micro in range(micro_count):
        slot_place, source, filled = slot_table(cold_routes[micro], axis_width, capacity)
        rows_out = tokens[micro][source // picks]
        rows_out = jnp.where(filled[:, None], rows_out, jnp.zeros_like(rows_out))
        outbound.append(rows_out.reshape(axis_width, capacity, model_width))
        tables.append(slot_place)
    joined = jnp.concatenate(outbound, axis=1)
    back_all = lax.all_to_all(
        expert_rows(
            lax.all_to_all(joined, "expert", split_axis=0, concat_axis=0, tiled=True), own_weights
        ),
        "expert",
        split_axis=0,
        concat_axis=0,
        tiled=True,
    )
    returned = [
        back_all[:, micro * capacity : (micro + 1) * capacity] for micro in range(micro_count)
    ]
    cold_parts = []
    for micro in range(micro_count):
        picked = returned[micro].reshape(axis_width * capacity, model_width)[tables[micro]]
        picked = picked.reshape(local_tokens, picks, model_width).astype(jnp.float32)
        cold_parts.append(jnp.sum(picked * gates[micro, :, 1:, None], axis=1))
    cold_total = jnp.stack(cold_parts)
    all_rows = micro_count * local_tokens
    flat = tokens.reshape(all_rows, model_width)
    order = jnp.argsort(hot_pick.reshape(all_rows), stable=True)
    share = all_rows // HOT
    grouped = flat[order].reshape(HOT, share, model_width)
    gate = jnp.einsum(
        "hsd,hdf->hsf",
        grouped,
        lax.all_gather(hot_gate, "expert", axis=2, tiled=True),
        preferred_element_type=jnp.float32,
    )
    upward = jnp.einsum(
        "hsd,hdf->hsf",
        grouped,
        lax.all_gather(hot_up, "expert", axis=2, tiled=True),
        preferred_element_type=jnp.float32,
    )
    hidden = (jax.nn.silu(gate) * upward).astype(jnp.bfloat16)
    hot_sum = jnp.einsum(
        "hsf,hdf->hsd",
        hidden,
        lax.all_gather(hot_down, "expert", axis=2, tiled=True),
        preferred_element_type=jnp.float32,
    )
    sorted_out = hot_sum.astype(jnp.bfloat16).reshape(all_rows, model_width)
    inverse = jnp.argsort(order)
    hot_out = sorted_out[inverse].astype(jnp.float32) * gates[:, :, 0].reshape(all_rows)[:, None]
    total = hot_out.reshape(micro_count, local_tokens, model_width) + cold_total
    return total.astype(jnp.bfloat16)


(
    CROSS_FIRST, SEND_Z, SEND_Y, SEND_CORE, PASS_Z, PASS_CORE, RELAY_OWN, RELAY_SIDE,
    RELAY_CORE, CROSS, REDUCE_SIDE, REDUCE_FAR, REDUCE_NEAR, FINISH_SIDE, FINISH_OWN, STEP,
) = range(16)
OWN, SIDE, FROM_Y, CORE_OWN, CORE_SIDE, SHARE_OWN, SHARE_SIDE, SUM_Y, SUM_Z = range(9)
AHEAD, BEHIND = range(2)
CHUNKS = 8
NEAR_IN = 7
NEAR_OUT = 4
HIGH = (7, 6, 5, 4)
LOW = (3, 2, 1, 0)
STEPS = 6
TABLE_WITH = 4
UNITS = (
    ((1, 0), (2, 0), (0, 1), (3, 0), (3, 1), (2, 1), (1, 1), (0, 0)),
    ((1, 0), (2, 0), (0, 0), (3, 0), (0, 1), (3, 1), (2, 1), (1, 1)),
)
OUTER = (
    (SEND_Z, 5, AHEAD), (SEND_Y, 1), (SEND_CORE,), (SEND_Z, 7, AHEAD), (SEND_Y, 6),
    (CROSS_FIRST,), (RELAY_OWN, 1, 6), (PASS_CORE, 1), (RELAY_OWN, 1, 4), (SEND_Z, 4, AHEAD),
    (PASS_CORE, 6), (SEND_Z, 6, AHEAD), (RELAY_OWN, 1, 5), (PASS_Z, 7), (SEND_Z, 3, AHEAD),
    (SEND_Z, 0, AHEAD), (SEND_Z, 2, AHEAD), (PASS_CORE, 7), (RELAY_OWN, 1, 7), (RELAY_CORE, 1, 6),
    (SEND_Y, 4), (SEND_Y, 0), (SEND_Y, 2), (SEND_Z, 1, AHEAD), (RELAY_OWN, 2, 6),
    (RELAY_CORE, 1, 4), (RELAY_SIDE, 1, 7), (RELAY_CORE, 1, 5), (STEP, 0, 0), (RELAY_OWN, 2, 4),
    (STEP, 0, 1), (RELAY_OWN, 2, 5), (STEP, 0, 2), (STEP, 0, 3), (RELAY_OWN, 3, 5), (SEND_Y, 3),
    (STEP, 0, 4), (STEP, 0, 5), (PASS_CORE, 2), (PASS_CORE, 4), (PASS_CORE, 0),
    (RELAY_CORE, 2, 6), (RELAY_SIDE, 2, 7), (RELAY_OWN, 3, 7), (REDUCE_FAR, 1, 5),
    (REDUCE_FAR, 1, 6), (REDUCE_FAR, 1, 4), (REDUCE_SIDE, 1, 7), (REDUCE_SIDE, 1, 6),
    (RELAY_CORE, 2, 4), (REDUCE_SIDE, 1, 4), (REDUCE_SIDE, 1, 5), (REDUCE_FAR, 1, 7),
    (RELAY_OWN, 2, 7), (RELAY_CORE, 2, 5), (RELAY_OWN, 3, 4), (SEND_Y, 5), (STEP, 1, 0),
    (RELAY_CORE, 3, 5), (RELAY_OWN, 2, 2), (STEP, 1, 1), (STEP, 1, 2), (RELAY_OWN, 1, 2),
    (STEP, 1, 3), (STEP, 1, 4), (STEP, 1, 5), (PASS_CORE, 3), (PASS_CORE, 5), (RELAY_CORE, 3, 4),
    (RELAY_OWN, 3, 6), (RELAY_OWN, 2, 1), (RELAY_CORE, 2, 2), (RELAY_OWN, 3, 0),
    (REDUCE_FAR, 2, 4), (REDUCE_FAR, 2, 5), (REDUCE_FAR, 2, 7), (REDUCE_SIDE, 2, 6),
    (REDUCE_SIDE, 2, 5), (REDUCE_SIDE, 2, 7), (REDUCE_SIDE, 2, 4), (STEP, 2, 0),
    (RELAY_CORE, 1, 2), (RELAY_OWN, 1, 0), (STEP, 2, 1), (STEP, 2, 2), (RELAY_CORE, 3, 6),
    (RELAY_SIDE, 3, 7), (STEP, 2, 3), (RELAY_OWN, 3, 2), (STEP, 2, 4), (STEP, 2, 5),
    (RELAY_OWN, 3, 3), (STEP, 3, 0), (RELAY_OWN, 3, 1), (STEP, 3, 1), (STEP, 3, 2),
    (RELAY_OWN, 1, 1), (RELAY_CORE, 3, 2), (STEP, 3, 3), (STEP, 3, 4), (RELAY_OWN, 2, 0),
    (RELAY_CORE, 3, 3), (STEP, 3, 5), (RELAY_CORE, 3, 1), (RELAY_OWN, 2, 3), (RELAY_CORE, 3, 0),
    (CROSS, 0, 2), (RELAY_CORE, 2, 1), (CROSS, 0, 1), (REDUCE_FAR, 2, 6), (CROSS, 0, 0),
    (CROSS, 0, 3), (RELAY_CORE, 1, 0), (REDUCE_FAR, 3, 7), (REDUCE_FAR, 3, 4), (RELAY_OWN, 1, 3),
    (REDUCE_FAR, 3, 5), (REDUCE_SIDE, 3, 4), (RELAY_CORE, 1, 1), (REDUCE_SIDE, 3, 6),
    (REDUCE_SIDE, 3, 7), (STEP, 4, 0), (STEP, 4, 1), (RELAY_CORE, 2, 0), (STEP, 4, 2),
    (RELAY_CORE, 2, 3), (STEP, 4, 3), (STEP, 4, 4), (STEP, 4, 5), (STEP, 5, 0), (STEP, 5, 1),
    (CROSS, 3, 2), (CROSS, 3, 0), (CROSS, 3, 3), (STEP, 5, 2), (STEP, 5, 3), (STEP, 5, 4),
    (RELAY_CORE, 1, 3), (STEP, 5, 5), (CROSS, 3, 1), (REDUCE_SIDE, 3, 5), (REDUCE_FAR, 3, 6),
    (REDUCE_NEAR, 3, 2), (STEP, 6, 0), (CROSS, 2, 3), (CROSS, 2, 2), (CROSS, 2, 1),
    (REDUCE_NEAR, 3, 0), (CROSS, 2, 0), (STEP, 6, 1), (STEP, 6, 2), (REDUCE_NEAR, 3, 3),
    (STEP, 6, 3), (STEP, 6, 4), (REDUCE_NEAR, 3, 1), (STEP, 6, 5), (REDUCE_NEAR, 2, 3),
    (STEP, 7, 0), (STEP, 7, 1), (CROSS, 1, 0), (CROSS, 1, 1), (CROSS, 1, 3), (CROSS, 1, 2),
    (REDUCE_NEAR, 2, 1), (STEP, 7, 2), (STEP, 7, 3), (REDUCE_NEAR, 2, 0), (STEP, 7, 4),
    (STEP, 7, 5), (REDUCE_NEAR, 2, 2), (REDUCE_NEAR, 1, 0), (FINISH_SIDE, 0, 5),
    (REDUCE_NEAR, 1, 1), (FINISH_SIDE, 0, 4), (FINISH_SIDE, 0, 7), (FINISH_SIDE, 0, 6),
    (REDUCE_NEAR, 1, 3), (FINISH_OWN, 0, 2), (REDUCE_NEAR, 1, 2), (FINISH_OWN, 0, 0),
    (FINISH_OWN, 0, 5), (FINISH_OWN, 0, 3), (FINISH_OWN, 0, 4), (FINISH_OWN, 0, 1),
    (FINISH_OWN, 0, 7), (FINISH_OWN, 0, 6),
)
INNER = (
    (SEND_Z, 6, BEHIND), (SEND_Z, 6, AHEAD), (SEND_Z, 4, BEHIND), (SEND_CORE,),
    (SEND_Z, 5, BEHIND), (CROSS_FIRST,), (SEND_Y, 4), (SEND_Y, 6), (SEND_Z, 4, AHEAD),
    (SEND_Z, 5, AHEAD), (SEND_Y, 1), (SEND_Z, 7, BEHIND), (SEND_Y, 5), (RELAY_OWN, 0, 5),
    (RELAY_OWN, 2, 6), (PASS_Z, 7), (SEND_Z, 2, AHEAD), (PASS_CORE, 7), (RELAY_OWN, 2, 4),
    (RELAY_OWN, 0, 7), (PASS_CORE, 4), (RELAY_OWN, 2, 5), (PASS_CORE, 6), (SEND_Z, 7, AHEAD),
    (RELAY_OWN, 3, 5), (PASS_CORE, 1), (RELAY_OWN, 0, 4), (RELAY_SIDE, 2, 7), (PASS_CORE, 5),
    (RELAY_OWN, 0, 6), (STEP, 0, 0), (STEP, 0, 1), (RELAY_SIDE, 0, 7), (RELAY_OWN, 3, 7),
    (STEP, 0, 2), (SEND_Z, 1, AHEAD), (STEP, 0, 3), (RELAY_OWN, 2, 7), (RELAY_CORE, 2, 4),
    (STEP, 0, 4), (RELAY_OWN, 0, 0), (RELAY_OWN, 3, 4), (STEP, 0, 5), (RELAY_CORE, 2, 5),
    (RELAY_OWN, 0, 2), (RELAY_CORE, 2, 6), (RELAY_OWN, 0, 3), (RELAY_CORE, 0, 5),
    (RELAY_OWN, 2, 2), (SEND_Z, 2, BEHIND), (RELAY_OWN, 3, 6), (RELAY_CORE, 3, 5),
    (RELAY_OWN, 0, 1), (SEND_Z, 3, AHEAD), (STEP, 1, 0), (RELAY_CORE, 0, 4), (STEP, 1, 1),
    (RELAY_OWN, 2, 1), (STEP, 1, 2), (STEP, 1, 3), (RELAY_OWN, 3, 0), (STEP, 1, 4),
    (SEND_Z, 0, AHEAD), (RELAY_CORE, 0, 0), (SEND_Z, 0, BEHIND), (STEP, 1, 5), (RELAY_CORE, 0, 6),
    (RELAY_SIDE, 3, 7), (RELAY_CORE, 3, 4), (RELAY_OWN, 3, 2), (SEND_Y, 3), (RELAY_OWN, 3, 3),
    (RELAY_CORE, 0, 2), (STEP, 2, 0), (RELAY_OWN, 3, 1), (STEP, 2, 1), (RELAY_CORE, 0, 3),
    (STEP, 2, 2), (RELAY_CORE, 2, 2), (STEP, 2, 3), (SEND_Z, 1, BEHIND), (STEP, 2, 4),
    (RELAY_CORE, 3, 6), (STEP, 2, 5), (RELAY_OWN, 2, 0), (SEND_Y, 0), (RELAY_OWN, 2, 3),
    (SEND_Z, 3, BEHIND), (SEND_Y, 2), (RELAY_CORE, 0, 1), (STEP, 3, 0), (STEP, 3, 1),
    (STEP, 3, 2), (STEP, 3, 3), (REDUCE_FAR, 2, 4), (STEP, 3, 4), (RELAY_CORE, 3, 2),
    (STEP, 3, 5), (STEP, 4, 0), (REDUCE_FAR, 2, 7), (STEP, 4, 1), (REDUCE_SIDE, 2, 6),
    (STEP, 4, 2), (RELAY_CORE, 3, 1), (STEP, 4, 3), (REDUCE_SIDE, 2, 5), (STEP, 4, 4),
    (REDUCE_SIDE, 2, 7), (RELAY_CORE, 2, 0), (STEP, 4, 5), (PASS_CORE, 0), (REDUCE_FAR, 2, 5),
    (RELAY_CORE, 3, 3), (PASS_CORE, 3), (RELAY_CORE, 3, 0), (RELAY_CORE, 2, 1),
    (REDUCE_SIDE, 2, 4), (FINISH_SIDE, 1, 6), (CROSS, 0, 2), (RELAY_CORE, 2, 3), (CROSS, 0, 1),
    (CROSS, 0, 3), (CROSS, 0, 0), (REDUCE_FAR, 2, 6), (STEP, 5, 0), (FINISH_SIDE, 1, 5),
    (STEP, 5, 1), (FINISH_SIDE, 1, 7), (REDUCE_FAR, 3, 7), (STEP, 5, 2), (REDUCE_FAR, 3, 4),
    (STEP, 5, 3), (STEP, 5, 4), (STEP, 5, 5), (REDUCE_SIDE, 3, 4), (STEP, 6, 0),
    (REDUCE_FAR, 0, 7), (REDUCE_SIDE, 3, 6), (CROSS, 3, 0), (CROSS, 3, 2), (CROSS, 3, 1),
    (STEP, 6, 1), (REDUCE_SIDE, 3, 7), (STEP, 6, 2), (STEP, 6, 3), (REDUCE_SIDE, 0, 4),
    (STEP, 6, 4), (STEP, 6, 5), (FINISH_OWN, 1, 7), (CROSS, 3, 3), (REDUCE_FAR, 0, 4),
    (REDUCE_SIDE, 3, 5), (FINISH_OWN, 1, 6), (REDUCE_SIDE, 0, 7), (FINISH_SIDE, 1, 4),
    (PASS_CORE, 2), (REDUCE_SIDE, 0, 6), (FINISH_OWN, 1, 5), (REDUCE_FAR, 3, 5), (CROSS, 2, 3),
    (CROSS, 2, 1), (CROSS, 2, 0), (CROSS, 2, 2), (REDUCE_FAR, 3, 6), (STEP, 7, 0), (STEP, 7, 1),
    (REDUCE_NEAR, 3, 2), (STEP, 7, 2), (REDUCE_NEAR, 3, 0), (REDUCE_SIDE, 0, 5), (STEP, 7, 3),
    (REDUCE_FAR, 0, 5), (STEP, 7, 4), (REDUCE_NEAR, 3, 3), (STEP, 7, 5), (REDUCE_FAR, 0, 6),
    (REDUCE_NEAR, 3, 1), (FINISH_OWN, 1, 4), (REDUCE_NEAR, 0, 2), (REDUCE_NEAR, 2, 3),
    (CROSS, 1, 0), (CROSS, 1, 2), (CROSS, 1, 1), (CROSS, 1, 3), (REDUCE_NEAR, 0, 0),
    (REDUCE_NEAR, 2, 1), (REDUCE_NEAR, 0, 3), (REDUCE_NEAR, 2, 0), (REDUCE_NEAR, 0, 1),
    (REDUCE_NEAR, 2, 2), (FINISH_OWN, 1, 1), (FINISH_OWN, 1, 0), (FINISH_OWN, 1, 3),
    (FINISH_OWN, 1, 2),
)
ROOM = 56 * 2**20


def tile_of(extent, most):
    return most if extent % most == 0 else extent


def needs(q, nz, task):
    name, *at = task
    if name in (CROSS_FIRST, SEND_Z, SEND_Y, SEND_CORE):
        return []
    if name in (PASS_Z, PASS_CORE):
        return [(FROM_Y, q, at[0])]
    p, k = at
    if name == RELAY_OWN:
        return [(OWN, p, k)]
    if name == RELAY_SIDE:
        return [(SIDE, p, k)]
    if name == RELAY_CORE:
        return [(FROM_Y, p, k)]
    h = 0 if k >= CHUNKS // 2 else 1
    own, side = ([(share, p, h, t) for t in range(2)] for share in (SHARE_OWN, SHARE_SIDE))
    if p == q:
        came = [w for w, there in ((AHEAD, q > 0), (BEHIND, q < nz - 1)) if there]
    else:
        came = [w for w, there in ((AHEAD, p > q > 0), (BEHIND, p < q < nz - 1)) if there]
    far = [(SUM_Z, p, CHUNKS + k - NEAR_OUT, w) for w in came]
    mine = [(SUM_Z, p, k, w) for w in came]
    cross = [(SUM_Y, p, k)]
    return {
        CROSS: side, REDUCE_SIDE: side + far, FINISH_SIDE: side + far,
        REDUCE_FAR: own + mine, REDUCE_NEAR: own + cross + mine, FINISH_OWN: own + cross + mine,
    }[name]


def hooks(q, nz, tasks):
    at, waited = (-1, STEPS - 1), set()
    plan = {at: []}

    def fresh(keys):
        news = [key for key in keys if key not in waited]
        waited.update(news)
        return news

    for task in tasks:
        if task[0] != STEP:
            plan[at].append((fresh(needs(q, nz, task)), task))
            continue
        if task[2] == 0:
            p, h = UNITS[q][task[1]]
            half = range(CHUNKS // 2, CHUNKS) if h == 0 else range(CHUNKS // 2)
            half = {*half, TABLE_WITH}
            keys = [(core, p, k) for core in (CORE_OWN, CORE_SIDE) for k in half]
            keys += [(FROM_Y, p, k) for k in half if p == q or k < NEAR_IN]
            if p != q:
                keys += [(OWN, p, k) for k in half]
                keys += [(SIDE, p, k) for k in half if k >= NEAR_IN]
            plan[at].append((fresh(keys), None))
        at = (task[1], task[2])
        plan[at] = []
    return plan


def fused(
    n, hot, part, tok, routes, pick, gts, wg_in, wu_in, wd_in, hg_in, hu_in, hd_in, out,
    xs, keep, sc, rc, sy, ry, sz, rz, wg, wu, wd, wh, hid, hhid, table, gw,
    wsem, tsem, tu_s, td_s, tz_r, ty_s, ty_r, tc_s, tc_r, up_s, down_s, z_r, y_s, y_r, c_s, c_r,
    rc_s, rc_r, ry_s, ry_r, rz_s, rz_r,
):
    nz = n // 4
    rows, model = tok.shape
    units = wg.shape[1]
    pad = hhid.shape[1]
    piece = rows // CHUNKS
    half = rows // 2
    wide = units // 3
    band = model // 2
    tile = tile_of(band, 512)
    me = lax.axis_index("expert")
    c = lax.rem(me, 2)
    y = lax.rem(lax.div(me, 2), 2)
    z = lax.div(me, 4)
    own = y * 2 + c
    side = (1 - y) * 2 + c
    peer_y = z * 4 + side
    peer_c = z * 4 + y * 2 + (1 - c)
    outer = (z == 0) | (z == nz - 1)
    low = z * 2 < nz

    def plane(p):
        return jnp.where(low, p, nz - 1 - p)

    ahead = me + jnp.where(low, 4, -4)
    behind = me - jnp.where(low, 4, -4)

    def remote(src, dst, send, recv, device):
        return pltpu.make_async_remote_copy(
            src_ref=src, dst_ref=dst, send_sem=send, recv_sem=recv,
            device_id={"expert": device}, device_id_type=pl.DeviceIdType.MESH,
        )

    def span(k):
        return pl.ds(k * piece, piece)

    loads = [
        pltpu.make_async_copy(src, dst, wsem.at[i])
        for i, (src, dst) in enumerate((
            *(
                (src.at[h], wh.at[pl.ds(t * pad + h * part, part)])
                for t, src in enumerate((hg_in, hu_in, hd_in)) for h in range(hot)
            ),
            (wg_in, wg), (wu_in, wu), (wd_in, wd),
        ))
    ]
    first = pltpu.make_async_copy(tok, xs.at[z, own], tsem)
    first.start()
    barrier = pltpu.get_barrier_semaphore()

    def greet(device):
        pl.semaphore_signal(
            barrier, inc=1, device_id={"expert": device},
            device_id_type=pl.DeviceIdType.MESH,
        )

    greet(peer_c)
    greet(peer_y)
    greet(ahead)

    @pl.when(jnp.logical_not(outer))
    def _():
        greet(behind)

    table[me] = jnp.zeros(table.shape[1:], jnp.float32)
    micros = gts.shape[0]

    def joined(parts):
        return jnp.concatenate(parts, axis=1)

    warm_row = joined([gts[m, 0:1, :] for m in range(micros)])
    chosen = joined([pick[m : m + 1, :] for m in range(micros)])
    named = [
        (
            joined([routes[k, m : m + 1, :] for m in range(micros)]),
            joined([gts[m, k + 1 : k + 2, :] for m in range(micros)]),
        )
        for k in range(routes.shape[0])
    ]

    def row(e):
        return sum(jnp.where(route == e, weight, 0.0) for route, weight in named)

    for e in range(n):
        table[me, e : e + 1, :] = row(e)
    for h in range(hot):
        table[me, n + h : n + h + 1, :] = jnp.where(chosen == h, warm_row, 0.0)

    first.wait()
    for load in loads:
        load.start()
    pl.semaphore_wait(barrier, jnp.where(outer, 3, 4))

    def table_z(way, p):
        ref = table.at[plane(p) * 4 + own]
        send = tu_s if way == AHEAD else td_s
        return remote(
            ref, ref, send.at[plane(p)], tz_r.at[plane(p)], ahead if way == AHEAD else behind
        )

    def table_y(p):
        ref = table.at[plane(p) * 4 + own]
        return remote(ref, ref, ty_s.at[plane(p)], ty_r.at[plane(p)], peer_y)

    def table_c(p, which):
        ref = table.at[plane(p) * 4 + (own, side)[which]]
        return remote(ref, ref, tc_s.at[plane(p), which], tc_r.at[plane(p), which], peer_c)

    def go_z(way, p, slot, k):
        at = k if slot is own else CHUNKS + k - NEAR_IN
        ref = xs.at[plane(p), slot, span(k)]
        send = up_s if way == AHEAD else down_s
        return remote(
            ref, ref, send.at[plane(p), at], z_r.at[plane(p), at],
            ahead if way == AHEAD else behind,
        )

    def go_y(p, k):
        ref = xs.at[plane(p), own, span(k)]
        return remote(ref, ref, y_s.at[plane(p), k], y_r.at[plane(p), k], peer_y)

    def go_c(p, which, k):
        ref = xs.at[plane(p), (own, side)[which], span(k)]
        return remote(
            ref, ref, c_s.at[plane(p), which, k], c_r.at[plane(p), which, k], peer_c
        )

    def share(at, h, j, t):
        lines = pl.ds(pl.multiple_of((1 - h) * half, half), half)
        cols = pl.ds(t * band, band)
        return remote(
            sc.at[at, j, lines, cols], rc.at[at, j, lines, cols],
            rc_s.at[at, h, j, t], rc_r.at[at, h, j, t], peer_c,
        )

    def share_y(p, k):
        at = plane(p)
        return remote(
            sy.at[at, span(k)], ry.at[at, span(k)], ry_s.at[at, k], ry_r.at[at, k], peer_y
        )

    def landing(way, p, last):
        if not last:
            return plane(p)
        return jnp.where(low == (way == AHEAD), plane(p), nz)

    def share_z(way, q, p, at):
        slot = landing(way, p, p == (q + 1 if way == AHEAD else q - 1))
        return remote(
            sz.at[plane(p), span(at)], rz.at[slot, span(at)],
            rz_s.at[plane(p), at], rz_r.at[slot, at],
            ahead if way == AHEAD else behind,
        )

    def await_event(q, key):
        name, p, k, *rest = key
        tabled = k == TABLE_WITH
        if name == OWN:
            if tabled:
                table_z(AHEAD, p).wait_recv()
            go_z(AHEAD, p, own, k).wait_recv()
        elif name == SIDE:
            go_z(AHEAD, p, side, k).wait_recv()
        elif name == FROM_Y:
            if tabled:
                table_y(p).wait_recv()
            ref = xs.at[plane(p), side, span(k)]
            remote(ref, ref, y_s.at[plane(p), k], y_r.at[plane(p), k], peer_y).wait_recv()
        elif name in (CORE_OWN, CORE_SIDE):
            if tabled:
                table_c(p, int(name == CORE_SIDE)).wait_recv()
            go_c(p, int(name == CORE_SIDE), k).wait_recv()
        elif name in (SHARE_OWN, SHARE_SIDE):
            share(plane(p), k, y if name == SHARE_OWN else 1 - y, rest[0]).wait_recv()
        elif name == SUM_Y:
            share_y(p, k).wait_recv()
        else:
            slot = landing(rest[0], p, p == q)
            ref = rz.at[slot, span(k)]
            remote(ref, ref, rz_s.at[0, k], rz_r.at[slot, k], me).wait_recv()

    def ways(q, p):
        return (AHEAD,) * (p <= q and q + 1 < nz) + (BEHIND,) * (p >= q and q > 0)

    def add_up(dst, lines, terms):
        @pl.loop(0, model // tile)
        def _(t):
            cols = pl.ds(pl.multiple_of(t * tile, tile), tile)
            total = None
            for term in terms:
                value = term(cols).astype(jnp.float32)
                total = value if total is None else total + value
            dst[lines, cols] = total.astype(jnp.bfloat16)

    def act(q, task):
        name, *at = task
        if name == CROSS_FIRST:
            for k in HIGH + LOW:
                if k >= NEAR_IN:
                    go_y(q, k).start()
        elif name == SEND_Z:
            if at[0] == TABLE_WITH:
                table_z(at[1], q).start()
            go_z(at[1], q, own, at[0]).start()
        elif name == SEND_CORE:
            table_c(q, 0).start()
            for k in range(CHUNKS):
                go_c(q, 0, k).start()
        elif name == PASS_Z:
            for way in ways(q, q):
                go_z(way, q, side, at[0]).start()
        elif name == SEND_Y:
            if at[0] == TABLE_WITH:
                table_y(q).start()
            go_y(q, at[0]).start()
        elif name == PASS_CORE:
            if at[0] == TABLE_WITH:
                table_c(q, 1).start()
            go_c(q, 1, at[0]).start()
        elif name == RELAY_OWN:
            p, k = at
            if k == TABLE_WITH:
                for way in ways(q, p):
                    table_z(way, p).start()
                table_y(p).start()
                table_c(p, 0).start()
            for way in ways(q, p):
                go_z(way, p, own, k).start()
            if k < NEAR_IN:
                go_y(p, k).start()
            go_c(p, 0, k).start()
        elif name == RELAY_SIDE:
            p, k = at
            for way in ways(q, p):
                go_z(way, p, side, k).start()
            go_c(p, 1, k).start()
        elif name == RELAY_CORE:
            if at[1] == TABLE_WITH:
                table_c(at[0], 1).start()
            go_c(at[0], 1, at[1]).start()
        else:
            p, k = at
            j = 1 - y if name in (CROSS, REDUCE_SIDE, FINISH_SIDE) else y
            here = plane(p)
            terms = [
                lambda cols: keep[here, j, span(k), cols],
                lambda cols: rc[here, j, span(k), cols],
            ]
            for key in needs(q, nz, task):
                if key[0] == SUM_Y:
                    terms.append(lambda cols: ry[here, span(k), cols])
                if key[0] == SUM_Z:
                    slot, line = landing(key[3], p, p == q), span(key[2])
                    terms.append(lambda cols, slot=slot, line=line: rz[slot, line, cols])
            if name in (CROSS, FINISH_SIDE):
                add_up(sy.at[here], span(k), terms)
                share_y(p, k).start()
            elif name == FINISH_OWN:
                add_up(out, span(k), terms)
            else:
                line = CHUNKS + k - NEAR_OUT if name == REDUCE_SIDE else k
                add_up(sz.at[here], span(line), terms)
                share_z(AHEAD if p > q else BEHIND, q, p, line).start()

    plans = [hooks(q, nz, tasks) for q, tasks in enumerate((OUTER, INNER))]

    def perform(q, steps):
        for keys, task in steps:
            for key in keys:
                await_event(q, key)
            if task is not None:
                act(q, task)

    def by_class(emit):
        @pl.when(outer)
        def _():
            emit(0)

        @pl.when(jnp.logical_not(outer))
        def _():
            emit(1)

    count = len(UNITS[0])

    def hook(u, step):
        def emit(q):
            for j in range(count):
                if (j, step) != (count - 1, STEPS - 1) and plans[q].get((j, step)):
                    @pl.when(u == j)
                    def _():
                        perform(q, plans[q][j, step])

        by_class(emit)

    def picked(u, field):
        found = [
            functools.reduce(
                lambda rest, j: jnp.where(u == j, UNITS[q][j][field], rest),
                range(1, count), jnp.int32(UNITS[q][0][field]),
            )
            for q in range(2)
        ]
        return jnp.where(outer, *found)

    def take_weights():
        if pad > hot * part:
            for t in range(3):
                blank = wh.at[pl.ds(t * pad + hot * part, pad - hot * part)]
                blank[...] = jnp.zeros_like(blank)

        for load in loads:
            load.wait()

    def start(q):
        for keys, task in plans[q][-1, STEPS - 1]:
            if task is None:
                take_weights()
            perform(q, [(keys, task)])

    by_class(start)

    @pl.loop(0, count)
    def _(u):
        here = plane(picked(u, 0))
        h = picked(u, 1)
        lines = pl.ds(pl.multiple_of((1 - h) * half, half), half)

        def block():
            return xs[here, :, lines, :].reshape(4 * half, model)

        for j in range(4):
            given = [table[here * 4 + j, pl.ds(me, 1), :]]
            given += [table[here * 4 + j, n + i : n + i + 1, :] for i in range(hot)]
            given.append(jnp.zeros((8 - len(given), rows), jnp.float32))
            gw[j] = jnp.transpose(jnp.concatenate(given, axis=0))

        def columns(which):
            return jnp.concatenate(
                [gw[j, lines, which : which + 1] for j in range(4)], axis=0
            )

        for i in range(3):
            cols = pl.ds(i * wide, wide)
            v = block()
            g = jnp.dot(v, wg[:, cols], preferred_element_type=jnp.float32)
            up = jnp.dot(v, wu[:, cols], preferred_element_type=jnp.float32)
            hid[:, cols] = (g / (1.0 + jnp.exp(-g)) * up).astype(jnp.bfloat16)
            hook(u, i)

        gu = lax.dot_general(
            block(), wh[: 2 * pad, :], (((1,), (1,)), ((), ())),
            preferred_element_type=jnp.float32,
        )
        g, up = gu[:, :pad], gu[:, pad:]
        lane = lax.broadcasted_iota(jnp.int32, (4 * half, pad), 1)
        warm = jnp.zeros((4 * half, pad), jnp.float32)
        for i in range(hot):
            warm = jnp.where((lane >= i * part) & (lane < (i + 1) * part), columns(1 + i), warm)
        hhid[...] = (g / (1.0 + jnp.exp(-g)) * up * warm).astype(jnp.bfloat16)
        hook(u, 3)

        cold = columns(0)
        for t in range(2):
            for i in range(band // tile):
                cols = pl.ds(t * band + i * tile, tile)
                r = jnp.dot(hid[...], wd[:, cols], preferred_element_type=jnp.float32)
                r = r.astype(jnp.bfloat16).astype(jnp.float32) * cold
                r = r + jnp.dot(
                    hhid[...], wh[2 * pad :, cols], preferred_element_type=jnp.float32
                )
                for j in range(2):
                    even = r[2 * j * half : (2 * j + 1) * half]
                    odd = r[(2 * j + 1) * half : (2 * j + 2) * half]
                    keep[here, j, lines, cols] = jnp.where(c == 0, even, odd)
                    sc[here, j, lines, cols] = jnp.where(c == 0, odd, even).astype(jnp.bfloat16)
            share(here, h, 1 - y, t).start()
            share(here, h, y, t).start()
            hook(u, 4 + t)

    by_class(lambda q: perform(q, plans[q][count - 1, STEPS - 1]))

    def settle(q):
        for p in range(nz):
            for way in ways(q, p):
                table_z(way, p).wait_send()
            table_y(p).wait_send()
            table_c(p, 0).wait_send()
            table_c(p, 1).wait_send()
            for k in range(CHUNKS):
                for way in ways(q, p):
                    go_z(way, p, own, k).wait_send()
                    if k >= NEAR_IN:
                        go_z(way, p, side, k).wait_send()
                if k < NEAR_IN or p == q:
                    go_y(p, k).wait_send()
                go_c(p, 0, k).wait_send()
                go_c(p, 1, k).wait_send()
                if k < NEAR_OUT or p == q:
                    share_y(p, k).wait_send()
            for h in range(2):
                for j in range(2):
                    for t in range(2):
                        share(plane(p), h, j, t).wait_send()
            if p != q:
                for at in range(2 * CHUNKS - NEAR_OUT):
                    share_z(AHEAD if p > q else BEHIND, q, p, at).wait_send()

    by_class(settle)


def scratch(n, rows, model, units, pad, hot):
    nz = n // 4
    half, full = jnp.bfloat16, jnp.float32
    dma = pltpu.SemaphoreType.DMA
    piece = rows // CHUNKS
    gathers, reduces = 2 * CHUNKS - NEAR_IN, 2 * CHUNKS - NEAR_OUT
    return [
        pltpu.VMEM((nz, 4, rows, model), half),
        pltpu.VMEM((nz, 2, rows, model), full),
        pltpu.VMEM((nz, 2, rows, model), half),
        pltpu.VMEM((nz, 2, rows, model), half),
        pltpu.VMEM((nz, rows, model), half),
        pltpu.VMEM((nz, rows, model), half),
        pltpu.VMEM((nz, reduces * piece, model), half),
        pltpu.VMEM((nz + 1, reduces * piece, model), half),
        pltpu.VMEM((model, units), half),
        pltpu.VMEM((model, units), half),
        pltpu.VMEM((units, model), half),
        pltpu.VMEM((3 * pad, model), half),
        pltpu.VMEM((2 * rows, units), half),
        pltpu.VMEM((2 * rows, pad), half),
        pltpu.VMEM((n, -(-(n + hot) // 8) * 8, rows), full),
        pltpu.VMEM((4, rows, 8), full),
        dma((3 + 3 * hot,)), dma, dma((nz,)), dma((nz,)), dma((nz,)),
        dma((nz,)), dma((nz,)), dma((nz, 2)), dma((nz, 2)),
        dma((nz, gathers)), dma((nz, gathers)), dma((nz, gathers)),
        dma((nz, CHUNKS)), dma((nz, CHUNKS)), dma((nz, 2, CHUNKS)), dma((nz, 2, CHUNKS)),
        dma((nz, 2, 2, 2)), dma((nz, 2, 2, 2)),
        dma((nz, CHUNKS)), dma((nz, CHUNKS)),
        dma((nz, reduces)), dma((nz + 1, reduces)),
    ]


def shards(tokens, w_gate, w_up, w_down, hot_gate, hot_up, hot_down, cold_routes, hot_pick, gates):
    n = lax.axis_size("expert")
    micro_count, local_tokens, model = tokens.shape
    rows = micro_count * local_tokens
    hot, units, part = hot_gate.shape[0], w_gate.shape[2], hot_gate.shape[2]
    pad = -(-hot * part // 128) * 128
    need = rows * model * n * 9 + 3 * model * (units + pad) * 2
    if n != 16 or part % 16 or rows % (16 * CHUNKS) or units % 384 or model % 256 or need > ROOM or hot > 7:
        return routed(
            tokens, w_gate, w_up, w_down, hot_gate, hot_up, hot_down, cold_routes, hot_pick, gates
        )
    anyplace = pl.BlockSpec(memory_space=pl.ANY)
    vmem = pl.BlockSpec(memory_space=pltpu.VMEM)
    mixed = pl.pallas_call(
        functools.partial(fused, n, hot, part),
        out_shape=jax.ShapeDtypeStruct((rows, model), jnp.bfloat16),
        in_specs=[anyplace, vmem, vmem, vmem] + [anyplace] * 6,
        out_specs=vmem,
        scratch_shapes=scratch(n, rows, model, units, pad, hot),
        compiler_params=pltpu.CompilerParams(
            collective_id=0, has_side_effects=True, vmem_limit_bytes=64 * 2**20 - 2**17
        ),
    )(
        tokens.reshape(rows, model), jnp.transpose(cold_routes, (2, 0, 1)), hot_pick,
        jnp.swapaxes(gates, 1, 2),
        w_gate[0], w_up[0], w_down[0],
        *(jnp.swapaxes(w, 1, 2) for w in (hot_gate, hot_up, hot_down)),
    )
    return mixed.reshape(tokens.shape)


def solution(mesh):
    in_specs = (
        P(None, ("groups", "expert"), None),
        P("expert", None, None),
        P("expert", None, None),
        P("expert", None, None),
        P(None, None, "expert"),
        P(None, None, "expert"),
        P(None, None, "expert"),
        P(None, ("groups", "expert"), None),
        P(None, ("groups", "expert")),
        P(None, ("groups", "expert"), None),
    )
    out_specs = P(None, ("groups", "expert"), None)
    return jax.shard_map(shards, mesh=mesh, in_specs=in_specs, out_specs=out_specs, check_vma=False)
```

```python
import functools

import jax
import jax.numpy as jnp
from jax import lax
from jax.experimental import pallas as pl
from jax.experimental.pallas import tpu as pltpu
from jax.sharding import PartitionSpec as P

TOP = 8
HOT = 2


def expert_rows(rows_in, weights):
    leading = rows_in.shape[:-1]
    flat_rows = rows_in.reshape(-1, rows_in.shape[-1])
    gate = jnp.dot(flat_rows, weights[0], preferred_element_type=jnp.float32)
    upward = jnp.dot(flat_rows, weights[1], preferred_element_type=jnp.float32)
    hidden = (jax.nn.silu(gate) * upward).astype(jnp.bfloat16)
    result = jnp.dot(hidden, weights[2], preferred_element_type=jnp.float32).astype(jnp.bfloat16)
    return result.reshape(leading + (result.shape[-1],))


def slot_table(routes_block, axis_width, capacity):
    expert = routes_block.reshape(-1)
    total_count = expert.shape[0]
    onehot = (expert[:, None] == jnp.arange(axis_width, dtype=jnp.int32)[None, :]).astype(jnp.int32)
    before = jnp.cumsum(onehot, axis=0) - onehot
    slot_rank = jnp.sum(before * onehot, axis=1)
    slot_place = expert * capacity + slot_rank
    target = jnp.arange(axis_width * capacity, dtype=jnp.int32)
    matched = slot_place[None, :] == target[:, None]
    filled = jnp.any(matched, axis=1)
    source = jnp.sum(
        jnp.where(matched, jnp.arange(total_count, dtype=jnp.int32)[None, :], 0), axis=1
    )
    return (slot_place, source, filled)


def routed(tokens, w_gate, w_up, w_down, hot_gate, hot_up, hot_down, cold_routes, hot_pick, gates):
    axis_width = lax.axis_size("expert")
    micro_count, local_tokens, model_width = tokens.shape
    picks = TOP - 1
    capacity = local_tokens * picks * 3 // (2 * axis_width) + 1
    own_weights = (w_gate[0], w_up[0], w_down[0])
    outbound = []
    tables = []
    for micro in range(micro_count):
        slot_place, source, filled = slot_table(cold_routes[micro], axis_width, capacity)
        rows_out = tokens[micro][source // picks]
        rows_out = jnp.where(filled[:, None], rows_out, jnp.zeros_like(rows_out))
        outbound.append(rows_out.reshape(axis_width, capacity, model_width))
        tables.append(slot_place)
    joined = jnp.concatenate(outbound, axis=1)
    back_all = lax.all_to_all(
        expert_rows(
            lax.all_to_all(joined, "expert", split_axis=0, concat_axis=0, tiled=True), own_weights
        ),
        "expert",
        split_axis=0,
        concat_axis=0,
        tiled=True,
    )
    returned = [
        back_all[:, micro * capacity : (micro + 1) * capacity] for micro in range(micro_count)
    ]
    cold_parts = []
    for micro in range(micro_count):
        picked = returned[micro].reshape(axis_width * capacity, model_width)[tables[micro]]
        picked = picked.reshape(local_tokens, picks, model_width).astype(jnp.float32)
        cold_parts.append(jnp.sum(picked * gates[micro, :, 1:, None], axis=1))
    cold_total = jnp.stack(cold_parts)
    all_rows = micro_count * local_tokens
    flat = tokens.reshape(all_rows, model_width)
    order = jnp.argsort(hot_pick.reshape(all_rows), stable=True)
    share = all_rows // HOT
    grouped = flat[order].reshape(HOT, share, model_width)
    gate = jnp.einsum(
        "hsd,hdf->hsf",
        grouped,
        lax.all_gather(hot_gate, "expert", axis=2, tiled=True),
        preferred_element_type=jnp.float32,
    )
    upward = jnp.einsum(
        "hsd,hdf->hsf",
        grouped,
        lax.all_gather(hot_up, "expert", axis=2, tiled=True),
        preferred_element_type=jnp.float32,
    )
    hidden = (jax.nn.silu(gate) * upward).astype(jnp.bfloat16)
    hot_sum = jnp.einsum(
        "hsf,hdf->hsd",
        hidden,
        lax.all_gather(hot_down, "expert", axis=2, tiled=True),
        preferred_element_type=jnp.float32,
    )
    sorted_out = hot_sum.astype(jnp.bfloat16).reshape(all_rows, model_width)
    inverse = jnp.argsort(order)
    hot_out = sorted_out[inverse].astype(jnp.float32) * gates[:, :, 0].reshape(all_rows)[:, None]
    total = hot_out.reshape(micro_count, local_tokens, model_width) + cold_total
    return total.astype(jnp.bfloat16)


(
    CROSS_FIRST, SEND_Z, SEND_Y, SEND_CORE, PASS_Z, PASS_CORE, RELAY_OWN, RELAY_SIDE,
    RELAY_CORE, CROSS, REDUCE_SIDE, REDUCE_FAR, REDUCE_NEAR, FINISH_SIDE, FINISH_OWN, STEP,
) = range(16)
OWN, SIDE, FROM_Y, CORE_OWN, CORE_SIDE, SHARE_OWN, SHARE_SIDE, SUM_Y, SUM_Z = range(9)
AHEAD, BEHIND = range(2)
CHUNKS = 8
NEAR_IN = 7
NEAR_OUT = 4
HIGH = (7, 6, 5, 4)
LOW = (3, 2, 1, 0)
STEPS = 6
TABLE_WITH = 4
UNITS = (
    ((1, 0), (2, 0), (0, 1), (3, 0), (3, 1), (2, 1), (1, 1), (0, 0)),
    ((1, 0), (2, 0), (0, 0), (3, 0), (0, 1), (3, 1), (2, 1), (1, 1)),
)
OUTER = (
    (SEND_Z, 5, AHEAD), (SEND_Y, 1), (SEND_CORE,), (SEND_Z, 7, AHEAD), (SEND_Y, 6),
    (CROSS_FIRST,), (RELAY_OWN, 1, 6), (PASS_CORE, 1), (RELAY_OWN, 1, 4), (SEND_Z, 4, AHEAD),
    (PASS_CORE, 6), (SEND_Z, 6, AHEAD), (RELAY_OWN, 1, 5), (PASS_Z, 7), (SEND_Z, 3, AHEAD),
    (SEND_Z, 0, AHEAD), (SEND_Z, 2, AHEAD), (PASS_CORE, 7), (RELAY_OWN, 1, 7), (RELAY_CORE, 1, 6),
    (SEND_Y, 4), (SEND_Y, 0), (SEND_Y, 2), (SEND_Z, 1, AHEAD), (RELAY_OWN, 2, 6),
    (RELAY_CORE, 1, 4), (RELAY_SIDE, 1, 7), (RELAY_CORE, 1, 5), (STEP, 0, 0), (RELAY_OWN, 2, 4),
    (STEP, 0, 1), (RELAY_OWN, 2, 5), (STEP, 0, 2), (STEP, 0, 3), (RELAY_OWN, 3, 5), (SEND_Y, 3),
    (STEP, 0, 4), (STEP, 0, 5), (PASS_CORE, 2), (PASS_CORE, 4), (PASS_CORE, 0),
    (RELAY_CORE, 2, 6), (RELAY_SIDE, 2, 7), (RELAY_OWN, 3, 7), (REDUCE_FAR, 1, 5),
    (REDUCE_FAR, 1, 6), (REDUCE_FAR, 1, 4), (REDUCE_SIDE, 1, 7), (REDUCE_SIDE, 1, 6),
    (RELAY_CORE, 2, 4), (REDUCE_SIDE, 1, 4), (REDUCE_SIDE, 1, 5), (REDUCE_FAR, 1, 7),
    (RELAY_OWN, 2, 7), (RELAY_CORE, 2, 5), (RELAY_OWN, 3, 4), (SEND_Y, 5), (STEP, 1, 0),
    (RELAY_CORE, 3, 5), (RELAY_OWN, 2, 2), (STEP, 1, 1), (STEP, 1, 2), (RELAY_OWN, 1, 2),
    (STEP, 1, 3), (STEP, 1, 4), (STEP, 1, 5), (PASS_CORE, 3), (PASS_CORE, 5), (RELAY_CORE, 3, 4),
    (RELAY_OWN, 3, 6), (RELAY_OWN, 2, 1), (RELAY_CORE, 2, 2), (RELAY_OWN, 3, 0),
    (REDUCE_FAR, 2, 4), (REDUCE_FAR, 2, 5), (REDUCE_FAR, 2, 7), (REDUCE_SIDE, 2, 6),
    (REDUCE_SIDE, 2, 5), (REDUCE_SIDE, 2, 7), (REDUCE_SIDE, 2, 4), (STEP, 2, 0),
    (RELAY_CORE, 1, 2), (RELAY_OWN, 1, 0), (STEP, 2, 1), (STEP, 2, 2), (RELAY_CORE, 3, 6),
    (RELAY_SIDE, 3, 7), (STEP, 2, 3), (RELAY_OWN, 3, 2), (STEP, 2, 4), (STEP, 2, 5),
    (RELAY_OWN, 3, 3), (STEP, 3, 0), (RELAY_OWN, 3, 1), (STEP, 3, 1), (STEP, 3, 2),
    (RELAY_OWN, 1, 1), (RELAY_CORE, 3, 2), (STEP, 3, 3), (STEP, 3, 4), (RELAY_OWN, 2, 0),
    (RELAY_CORE, 3, 3), (STEP, 3, 5), (RELAY_CORE, 3, 1), (RELAY_OWN, 2, 3), (RELAY_CORE, 3, 0),
    (CROSS, 0, 2), (RELAY_CORE, 2, 1), (CROSS, 0, 1), (REDUCE_FAR, 2, 6), (CROSS, 0, 0),
    (CROSS, 0, 3), (RELAY_CORE, 1, 0), (REDUCE_FAR, 3, 7), (REDUCE_FAR, 3, 4), (RELAY_OWN, 1, 3),
    (REDUCE_FAR, 3, 5), (REDUCE_SIDE, 3, 4), (RELAY_CORE, 1, 1), (REDUCE_SIDE, 3, 6),
    (REDUCE_SIDE, 3, 7), (STEP, 4, 0), (STEP, 4, 1), (RELAY_CORE, 2, 0), (STEP, 4, 2),
    (RELAY_CORE, 2, 3), (STEP, 4, 3), (STEP, 4, 4), (STEP, 4, 5), (STEP, 5, 0), (STEP, 5, 1),
    (CROSS, 3, 2), (CROSS, 3, 0), (CROSS, 3, 3), (STEP, 5, 2), (STEP, 5, 3), (STEP, 5, 4),
    (RELAY_CORE, 1, 3), (STEP, 5, 5), (CROSS, 3, 1), (REDUCE_SIDE, 3, 5), (REDUCE_FAR, 3, 6),
    (REDUCE_NEAR, 3, 2), (STEP, 6, 0), (CROSS, 2, 3), (CROSS, 2, 2), (CROSS, 2, 1),
    (REDUCE_NEAR, 3, 0), (CROSS, 2, 0), (STEP, 6, 1), (STEP, 6, 2), (REDUCE_NEAR, 3, 3),
    (STEP, 6, 3), (STEP, 6, 4), (REDUCE_NEAR, 3, 1), (STEP, 6, 5), (REDUCE_NEAR, 2, 3),
    (STEP, 7, 0), (STEP, 7, 1), (CROSS, 1, 0), (CROSS, 1, 1), (CROSS, 1, 3), (CROSS, 1, 2),
    (REDUCE_NEAR, 2, 1), (STEP, 7, 2), (STEP, 7, 3), (REDUCE_NEAR, 2, 0), (STEP, 7, 4),
    (STEP, 7, 5), (REDUCE_NEAR, 2, 2), (REDUCE_NEAR, 1, 0), (FINISH_SIDE, 0, 5),
    (REDUCE_NEAR, 1, 1), (FINISH_SIDE, 0, 4), (FINISH_SIDE, 0, 7), (FINISH_SIDE, 0, 6),
    (REDUCE_NEAR, 1, 3), (FINISH_OWN, 0, 2), (REDUCE_NEAR, 1, 2), (FINISH_OWN, 0, 0),
    (FINISH_OWN, 0, 5), (FINISH_OWN, 0, 3), (FINISH_OWN, 0, 4), (FINISH_OWN, 0, 1),
    (FINISH_OWN, 0, 7), (FINISH_OWN, 0, 6),
)
INNER = (
    (SEND_Z, 6, BEHIND), (SEND_Z, 6, AHEAD), (SEND_Z, 4, BEHIND), (SEND_CORE,),
    (SEND_Z, 5, BEHIND), (CROSS_FIRST,), (SEND_Y, 4), (SEND_Y, 6), (SEND_Z, 4, AHEAD),
    (SEND_Z, 5, AHEAD), (SEND_Y, 1), (SEND_Z, 7, BEHIND), (SEND_Y, 5), (RELAY_OWN, 0, 5),
    (RELAY_OWN, 2, 6), (PASS_Z, 7), (SEND_Z, 2, AHEAD), (PASS_CORE, 7), (RELAY_OWN, 2, 4),
    (RELAY_OWN, 0, 7), (PASS_CORE, 4), (RELAY_OWN, 2, 5), (PASS_CORE, 6), (SEND_Z, 7, AHEAD),
    (RELAY_OWN, 3, 5), (PASS_CORE, 1), (RELAY_OWN, 0, 4), (RELAY_SIDE, 2, 7), (PASS_CORE, 5),
    (RELAY_OWN, 0, 6), (STEP, 0, 0), (STEP, 0, 1), (RELAY_SIDE, 0, 7), (RELAY_OWN, 3, 7),
    (STEP, 0, 2), (SEND_Z, 1, AHEAD), (STEP, 0, 3), (RELAY_OWN, 2, 7), (RELAY_CORE, 2, 4),
    (STEP, 0, 4), (RELAY_OWN, 0, 0), (RELAY_OWN, 3, 4), (STEP, 0, 5), (RELAY_CORE, 2, 5),
    (RELAY_OWN, 0, 2), (RELAY_CORE, 2, 6), (RELAY_OWN, 0, 3), (RELAY_CORE, 0, 5),
    (RELAY_OWN, 2, 2), (SEND_Z, 2, BEHIND), (RELAY_OWN, 3, 6), (RELAY_CORE, 3, 5),
    (RELAY_OWN, 0, 1), (SEND_Z, 3, AHEAD), (STEP, 1, 0), (RELAY_CORE, 0, 4), (STEP, 1, 1),
    (RELAY_OWN, 2, 1), (STEP, 1, 2), (STEP, 1, 3), (RELAY_OWN, 3, 0), (STEP, 1, 4),
    (SEND_Z, 0, AHEAD), (RELAY_CORE, 0, 0), (SEND_Z, 0, BEHIND), (STEP, 1, 5), (RELAY_CORE, 0, 6),
    (RELAY_SIDE, 3, 7), (RELAY_CORE, 3, 4), (RELAY_OWN, 3, 2), (SEND_Y, 3), (RELAY_OWN, 3, 3),
    (RELAY_CORE, 0, 2), (STEP, 2, 0), (RELAY_OWN, 3, 1), (STEP, 2, 1), (RELAY_CORE, 0, 3),
    (STEP, 2, 2), (RELAY_CORE, 2, 2), (STEP, 2, 3), (SEND_Z, 1, BEHIND), (STEP, 2, 4),
    (RELAY_CORE, 3, 6), (STEP, 2, 5), (RELAY_OWN, 2, 0), (SEND_Y, 0), (RELAY_OWN, 2, 3),
    (SEND_Z, 3, BEHIND), (SEND_Y, 2), (RELAY_CORE, 0, 1), (STEP, 3, 0), (STEP, 3, 1),
    (STEP, 3, 2), (STEP, 3, 3), (REDUCE_FAR, 2, 4), (STEP, 3, 4), (RELAY_CORE, 3, 2),
    (STEP, 3, 5), (STEP, 4, 0), (REDUCE_FAR, 2, 7), (STEP, 4, 1), (REDUCE_SIDE, 2, 6),
    (STEP, 4, 2), (RELAY_CORE, 3, 1), (STEP, 4, 3), (REDUCE_SIDE, 2, 5), (STEP, 4, 4),
    (REDUCE_SIDE, 2, 7), (RELAY_CORE, 2, 0), (STEP, 4, 5), (PASS_CORE, 0), (REDUCE_FAR, 2, 5),
    (RELAY_CORE, 3, 3), (PASS_CORE, 3), (RELAY_CORE, 3, 0), (RELAY_CORE, 2, 1),
    (REDUCE_SIDE, 2, 4), (FINISH_SIDE, 1, 6), (CROSS, 0, 2), (RELAY_CORE, 2, 3), (CROSS, 0, 1),
    (CROSS, 0, 3), (CROSS, 0, 0), (REDUCE_FAR, 2, 6), (STEP, 5, 0), (FINISH_SIDE, 1, 5),
    (STEP, 5, 1), (FINISH_SIDE, 1, 7), (REDUCE_FAR, 3, 7), (STEP, 5, 2), (REDUCE_FAR, 3, 4),
    (STEP, 5, 3), (STEP, 5, 4), (STEP, 5, 5), (REDUCE_SIDE, 3, 4), (STEP, 6, 0),
    (REDUCE_FAR, 0, 7), (REDUCE_SIDE, 3, 6), (CROSS, 3, 0), (CROSS, 3, 2), (CROSS, 3, 1),
    (STEP, 6, 1), (REDUCE_SIDE, 3, 7), (STEP, 6, 2), (STEP, 6, 3), (REDUCE_SIDE, 0, 4),
    (STEP, 6, 4), (STEP, 6, 5), (FINISH_OWN, 1, 7), (CROSS, 3, 3), (REDUCE_FAR, 0, 4),
    (REDUCE_SIDE, 3, 5), (FINISH_OWN, 1, 6), (REDUCE_SIDE, 0, 7), (FINISH_SIDE, 1, 4),
    (PASS_CORE, 2), (REDUCE_SIDE, 0, 6), (FINISH_OWN, 1, 5), (REDUCE_FAR, 3, 5), (CROSS, 2, 3),
    (CROSS, 2, 1), (CROSS, 2, 0), (CROSS, 2, 2), (REDUCE_FAR, 3, 6), (STEP, 7, 0), (STEP, 7, 1),
    (REDUCE_NEAR, 3, 2), (STEP, 7, 2), (REDUCE_NEAR, 3, 0), (REDUCE_SIDE, 0, 5), (STEP, 7, 3),
    (REDUCE_FAR, 0, 5), (STEP, 7, 4), (REDUCE_NEAR, 3, 3), (STEP, 7, 5), (REDUCE_FAR, 0, 6),
    (REDUCE_NEAR, 3, 1), (FINISH_OWN, 1, 4), (REDUCE_NEAR, 0, 2), (REDUCE_NEAR, 2, 3),
    (CROSS, 1, 0), (CROSS, 1, 2), (CROSS, 1, 1), (CROSS, 1, 3), (REDUCE_NEAR, 0, 0),
    (REDUCE_NEAR, 2, 1), (REDUCE_NEAR, 0, 3), (REDUCE_NEAR, 2, 0), (REDUCE_NEAR, 0, 1),
    (REDUCE_NEAR, 2, 2), (FINISH_OWN, 1, 1), (FINISH_OWN, 1, 0), (FINISH_OWN, 1, 3),
    (FINISH_OWN, 1, 2),
)
ROOM = 56 * 2**20


def tile_of(extent, most):
    return most if extent % most == 0 else extent


def needs(q, nz, task):
    name, *at = task
    if name in (CROSS_FIRST, SEND_Z, SEND_Y, SEND_CORE):
        return []
    if name in (PASS_Z, PASS_CORE):
        return [(FROM_Y, q, at[0])]
    p, k = at
    if name == RELAY_OWN:
        return [(OWN, p, k)]
    if name == RELAY_SIDE:
        return [(SIDE, p, k)]
    if name == RELAY_CORE:
        return [(FROM_Y, p, k)]
    h = 0 if k >= CHUNKS // 2 else 1
    own, side = ([(share, p, h, t) for t in range(2)] for share in (SHARE_OWN, SHARE_SIDE))
    if p == q:
        came = [w for w, there in ((AHEAD, q > 0), (BEHIND, q < nz - 1)) if there]
    else:
        came = [w for w, there in ((AHEAD, p > q > 0), (BEHIND, p < q < nz - 1)) if there]
    far = [(SUM_Z, p, CHUNKS + k - NEAR_OUT, w) for w in came]
    mine = [(SUM_Z, p, k, w) for w in came]
    cross = [(SUM_Y, p, k)]
    return {
        CROSS: side, REDUCE_SIDE: side + far, FINISH_SIDE: side + far,
        REDUCE_FAR: own + mine, REDUCE_NEAR: own + cross + mine, FINISH_OWN: own + cross + mine,
    }[name]


def hooks(q, nz, tasks):
    at, waited = (-1, STEPS - 1), set()
    plan = {at: []}

    def fresh(keys):
        news = [key for key in keys if key not in waited]
        waited.update(news)
        return news

    for task in tasks:
        if task[0] != STEP:
            plan[at].append((fresh(needs(q, nz, task)), task))
            continue
        if task[2] == 0:
            p, h = UNITS[q][task[1]]
            half = range(CHUNKS // 2, CHUNKS) if h == 0 else range(CHUNKS // 2)
            half = {*half, TABLE_WITH}
            keys = [(core, p, k) for core in (CORE_OWN, CORE_SIDE) for k in half]
            keys += [(FROM_Y, p, k) for k in half if p == q or k < NEAR_IN]
            if p != q:
                keys += [(OWN, p, k) for k in half]
                keys += [(SIDE, p, k) for k in half if k >= NEAR_IN]
            plan[at].append((fresh(keys), None))
        at = (task[1], task[2])
        plan[at] = []
    return plan


def fused(
    n, hot, part, tok, routes, pick, gts, wg_in, wu_in, wd_in, hg_in, hu_in, hd_in, out,
    xs, keep, sc, rc, sy, ry, sz, rz, wg, wu, wd, wh, hid, hhid, table, gw,
    wsem, tsem, tu_s, td_s, tz_r, ty_s, ty_r, tc_s, tc_r, up_s, down_s, z_r, y_s, y_r, c_s, c_r,
    rc_s, rc_r, ry_s, ry_r, rz_s, rz_r,
):
    nz = n // 4
    rows, model = tok.shape
    units = wg.shape[1]
    pad = hhid.shape[1]
    piece = rows // CHUNKS
    half = rows // 2
    wide = units // 3
    band = model // 2
    tile = tile_of(band, 512)
    me = lax.axis_index("expert")
    c = lax.rem(me, 2)
    y = lax.rem(lax.div(me, 2), 2)
    z = lax.div(me, 4)
    own = y * 2 + c
    side = (1 - y) * 2 + c
    peer_y = z * 4 + side
    peer_c = z * 4 + y * 2 + (1 - c)
    outer = (z == 0) | (z == nz - 1)
    low = z * 2 < nz

    def plane(p):
        return jnp.where(low, p, nz - 1 - p)

    ahead = me + jnp.where(low, 4, -4)
    behind = me - jnp.where(low, 4, -4)

    def remote(src, dst, send, recv, device):
        return pltpu.make_async_remote_copy(
            src_ref=src, dst_ref=dst, send_sem=send, recv_sem=recv,
            device_id={"expert": device}, device_id_type=pl.DeviceIdType.MESH,
        )

    def span(k):
        return pl.ds(k * piece, piece)

    loads = [
        pltpu.make_async_copy(src, dst, wsem.at[i])
        for i, (src, dst) in enumerate((
            *(
                (src.at[h], wh.at[pl.ds(t * pad + h * part, part)])
                for t, src in enumerate((hg_in, hu_in, hd_in)) for h in range(hot)
            ),
            (wg_in, wg), (wu_in, wu), (wd_in, wd),
        ))
    ]
    first = pltpu.make_async_copy(tok, xs.at[z, own], tsem)
    first.start()
    barrier = pltpu.get_barrier_semaphore()

    def greet(device):
        pl.semaphore_signal(
            barrier, inc=1, device_id={"expert": device},
            device_id_type=pl.DeviceIdType.MESH,
        )

    greet(peer_c)
    greet(peer_y)
    greet(ahead)

    @pl.when(jnp.logical_not(outer))
    def _():
        greet(behind)

    for load in loads:
        load.start()
    pl.semaphore_wait(barrier, jnp.where(outer, 3, 4))

    def table_z(way, p):
        ref = table.at[plane(p) * 4 + own]
        send = tu_s if way == AHEAD else td_s
        return remote(
            ref, ref, send.at[plane(p)], tz_r.at[plane(p)], ahead if way == AHEAD else behind
        )

    def table_y(p):
        ref = table.at[plane(p) * 4 + own]
        return remote(ref, ref, ty_s.at[plane(p)], ty_r.at[plane(p)], peer_y)

    def table_c(p, which):
        ref = table.at[plane(p) * 4 + (own, side)[which]]
        return remote(ref, ref, tc_s.at[plane(p), which], tc_r.at[plane(p), which], peer_c)

    def go_z(way, p, slot, k, fresh=False):
        at = k if slot is own else CHUNKS + k - NEAR_IN
        ref = xs.at[plane(p), slot, span(k)]
        send = up_s if way == AHEAD else down_s
        return remote(
            tok.at[span(k)] if fresh else ref, ref, send.at[plane(p), at], z_r.at[plane(p), at],
            ahead if way == AHEAD else behind,
        )

    def go_y(p, k, fresh=False):
        ref = xs.at[plane(p), own, span(k)]
        return remote(tok.at[span(k)] if fresh else ref, ref, y_s.at[plane(p), k], y_r.at[plane(p), k], peer_y)

    def go_c(p, which, k, fresh=False):
        ref = xs.at[plane(p), (own, side)[which], span(k)]
        return remote(
            tok.at[span(k)] if fresh else ref, ref, c_s.at[plane(p), which, k], c_r.at[plane(p), which, k], peer_c
        )

    def share(at, h, j, t):
        lines = pl.ds(pl.multiple_of((1 - h) * half, half), half)
        cols = pl.ds(t * band, band)
        return remote(
            sc.at[at, j, lines, cols], rc.at[at, j, lines, cols],
            rc_s.at[at, h, j, t], rc_r.at[at, h, j, t], peer_c,
        )

    def share_y(p, k):
        at = plane(p)
        return remote(
            sy.at[at, span(k)], ry.at[at, span(k)], ry_s.at[at, k], ry_r.at[at, k], peer_y
        )

    def landing(way, p, last):
        if not last:
            return plane(p)
        return jnp.where(low == (way == AHEAD), plane(p), nz)

    def share_z(way, q, p, at):
        slot = landing(way, p, p == (q + 1 if way == AHEAD else q - 1))
        return remote(
            sz.at[plane(p), span(at)], rz.at[slot, span(at)],
            rz_s.at[plane(p), at], rz_r.at[slot, at],
            ahead if way == AHEAD else behind,
        )

    def await_event(q, key):
        name, p, k, *rest = key
        tabled = k == TABLE_WITH
        if name == OWN:
            if tabled:
                table_z(AHEAD, p).wait_recv()
            go_z(AHEAD, p, own, k).wait_recv()
        elif name == SIDE:
            go_z(AHEAD, p, side, k).wait_recv()
        elif name == FROM_Y:
            if tabled:
                table_y(p).wait_recv()
            ref = xs.at[plane(p), side, span(k)]
            remote(ref, ref, y_s.at[plane(p), k], y_r.at[plane(p), k], peer_y).wait_recv()
        elif name in (CORE_OWN, CORE_SIDE):
            if tabled:
                table_c(p, int(name == CORE_SIDE)).wait_recv()
            go_c(p, int(name == CORE_SIDE), k).wait_recv()
        elif name in (SHARE_OWN, SHARE_SIDE):
            share(plane(p), k, y if name == SHARE_OWN else 1 - y, rest[0]).wait_recv()
        elif name == SUM_Y:
            share_y(p, k).wait_recv()
        else:
            slot = landing(rest[0], p, p == q)
            ref = rz.at[slot, span(k)]
            remote(ref, ref, rz_s.at[0, k], rz_r.at[slot, k], me).wait_recv()

    def ways(q, p):
        return (AHEAD,) * (p <= q and q + 1 < nz) + (BEHIND,) * (p >= q and q > 0)

    def add_up(dst, lines, terms):
        @pl.loop(0, model // tile)
        def _(t):
            cols = pl.ds(pl.multiple_of(t * tile, tile), tile)
            total = None
            for term in terms:
                value = term(cols).astype(jnp.float32)
                total = value if total is None else total + value
            dst[lines, cols] = total.astype(jnp.bfloat16)

    def act(q, task):
        name, *at = task
        if name == CROSS_FIRST:
            for k in HIGH + LOW:
                if k >= NEAR_IN:
                    go_y(q, k, fresh=True).start()
        elif name == SEND_Z:
            if at[0] == TABLE_WITH:
                table_z(at[1], q).start()
            go_z(at[1], q, own, at[0], fresh=True).start()
        elif name == SEND_CORE:
            for k in range(CHUNKS):
                go_c(q, 0, k, fresh=True).start()
        elif name == PASS_Z:
            for way in ways(q, q):
                go_z(way, q, side, at[0]).start()
        elif name == SEND_Y:
            if at[0] == TABLE_WITH:
                table_y(q).start()
                table_c(q, 0).start()
            go_y(q, at[0], fresh=True).start()
        elif name == PASS_CORE:
            if at[0] == TABLE_WITH:
                table_c(q, 1).start()
            go_c(q, 1, at[0]).start()
        elif name == RELAY_OWN:
            p, k = at
            if k == TABLE_WITH:
                for way in ways(q, p):
                    table_z(way, p).start()
                table_y(p).start()
                table_c(p, 0).start()
            for way in ways(q, p):
                go_z(way, p, own, k).start()
            if k < NEAR_IN:
                go_y(p, k).start()
            go_c(p, 0, k).start()
        elif name == RELAY_SIDE:
            p, k = at
            for way in ways(q, p):
                go_z(way, p, side, k).start()
            go_c(p, 1, k).start()
        elif name == RELAY_CORE:
            if at[1] == TABLE_WITH:
                table_c(at[0], 1).start()
            go_c(at[0], 1, at[1]).start()
        else:
            p, k = at
            j = 1 - y if name in (CROSS, REDUCE_SIDE, FINISH_SIDE) else y
            here = plane(p)
            terms = [
                lambda cols: keep[here, j, span(k), cols],
                lambda cols: rc[here, j, span(k), cols],
            ]
            for key in needs(q, nz, task):
                if key[0] == SUM_Y:
                    terms.append(lambda cols: ry[here, span(k), cols])
                if key[0] == SUM_Z:
                    slot, line = landing(key[3], p, p == q), span(key[2])
                    terms.append(lambda cols, slot=slot, line=line: rz[slot, line, cols])
            if name in (CROSS, FINISH_SIDE):
                add_up(sy.at[here], span(k), terms)
                share_y(p, k).start()
            elif name == FINISH_OWN:
                add_up(out, span(k), terms)
            else:
                line = CHUNKS + k - NEAR_OUT if name == REDUCE_SIDE else k
                add_up(sz.at[here], span(line), terms)
                share_z(AHEAD if p > q else BEHIND, q, p, line).start()

    plans = [hooks(q, nz, tasks) for q, tasks in enumerate((OUTER, INNER))]

    def perform(q, steps):
        for keys, task in steps:
            for key in keys:
                await_event(q, key)
            if task is not None:
                act(q, task)

    def by_class(emit):
        @pl.when(outer)
        def _():
            emit(0)

        @pl.when(jnp.logical_not(outer))
        def _():
            emit(1)

    count = len(UNITS[0])

    def hook(u, step):
        def emit(q):
            for j in range(count):
                if (j, step) != (count - 1, STEPS - 1) and plans[q].get((j, step)):
                    @pl.when(u == j)
                    def _():
                        perform(q, plans[q][j, step])

        by_class(emit)

    def picked(u, field):
        found = [
            functools.reduce(
                lambda rest, j: jnp.where(u == j, UNITS[q][j][field], rest),
                range(1, count), jnp.int32(UNITS[q][0][field]),
            )
            for q in range(2)
        ]
        return jnp.where(outer, *found)

    def take_weights():
        if pad > hot * part:
            for t in range(3):
                blank = wh.at[pl.ds(t * pad + hot * part, pad - hot * part)]
                blank[...] = jnp.zeros_like(blank)

        first.wait()
        for load in loads:
            load.wait()

    def fill_table():
        table[me] = jnp.zeros(table.shape[1:], jnp.float32)
        micros = gts.shape[0]

        def joined(parts):
            return jnp.concatenate(parts, axis=1)

        warm_row = joined([gts[m, 0:1, :] for m in range(micros)])
        chosen = joined([pick[m : m + 1, :] for m in range(micros)])
        named = [
            (
                joined([routes[k, m : m + 1, :] for m in range(micros)]),
                joined([gts[m, k + 1 : k + 2, :] for m in range(micros)]),
            )
            for k in range(routes.shape[0])
        ]

        def row(e):
            return sum(jnp.where(route == e, weight, 0.0) for route, weight in named)

        for e in range(n):
            table[me, e : e + 1, :] = row(e)
        for h in range(hot):
            table[me, n + h : n + h + 1, :] = jnp.where(chosen == h, warm_row, 0.0)

    def start(q):
        filled = False
        for keys, task in plans[q][-1, STEPS - 1]:
            if task is None:
                take_weights()
            elif task[0] in (SEND_Z, SEND_Y) and task[1] == TABLE_WITH and not filled:
                fill_table()
                filled = True
            perform(q, [(keys, task)])

    by_class(start)

    @pl.loop(0, count)
    def _(u):
        here = plane(picked(u, 0))
        h = picked(u, 1)
        lines = pl.ds(pl.multiple_of((1 - h) * half, half), half)

        slots = (c, 2 + c, 1 - c, 3 - c)

        def block():
            return jnp.concatenate([xs[here, slot, lines, :] for slot in slots], axis=0)

        for j, slot in enumerate(slots):
            given = [table[here * 4 + slot, pl.ds(me, 1), :]]
            given += [table[here * 4 + slot, n + i : n + i + 1, :] for i in range(hot)]
            given.append(jnp.zeros((8 - len(given), rows), jnp.float32))
            gw[j] = jnp.transpose(jnp.concatenate(given, axis=0))

        def columns(which):
            return jnp.concatenate(
                [gw[j, lines, which : which + 1] for j in range(4)], axis=0
            )

        for i in range(3):
            cols = pl.ds(i * wide, wide)
            v = block()
            g = jnp.dot(v, wg[:, cols], preferred_element_type=jnp.float32)
            up = jnp.dot(v, wu[:, cols], preferred_element_type=jnp.float32)
            hid[:, cols] = (g / (1.0 + jnp.exp(-g)) * up).astype(jnp.bfloat16)
            hook(u, i)

        gu = lax.dot_general(
            block(), wh[: 2 * pad, :], (((1,), (1,)), ((), ())),
            preferred_element_type=jnp.float32,
        )
        g, up = gu[:, :pad], gu[:, pad:]
        lane = lax.broadcasted_iota(jnp.int32, (4 * half, pad), 1)
        warm = jnp.zeros((4 * half, pad), jnp.float32)
        for i in range(hot):
            warm = jnp.where((lane >= i * part) & (lane < (i + 1) * part), columns(1 + i), warm)
        hhid[...] = (g / (1.0 + jnp.exp(-g)) * up * warm).astype(jnp.bfloat16)
        hook(u, 3)

        cold = columns(0)
        for t in range(2):
            for i in range(band // tile):
                cols = pl.ds(t * band + i * tile, tile)
                r = jnp.dot(hid[...], wd[:, cols], preferred_element_type=jnp.float32)
                r = r.astype(jnp.bfloat16).astype(jnp.float32) * cold
                r = r + jnp.dot(
                    hhid[...], wh[2 * pad :, cols], preferred_element_type=jnp.float32
                )
                for j in range(2):
                    keep[here, j, lines, cols] = r[j * half : (j + 1) * half]
                    sc[here, j, lines, cols] = r[(2 + j) * half : (3 + j) * half].astype(
                        jnp.bfloat16
                    )
            share(here, h, 1 - y, t).start()
            share(here, h, y, t).start()
            hook(u, 4 + t)

    by_class(lambda q: perform(q, plans[q][count - 1, STEPS - 1]))

    def settle(q):
        for p in range(nz):
            for way in ways(q, p):
                table_z(way, p).wait_send()
            table_y(p).wait_send()
            table_c(p, 0).wait_send()
            table_c(p, 1).wait_send()
            for k in range(CHUNKS):
                for way in ways(q, p):
                    go_z(way, p, own, k).wait_send()
                    if k >= NEAR_IN:
                        go_z(way, p, side, k).wait_send()
                if k < NEAR_IN or p == q:
                    go_y(p, k).wait_send()
                go_c(p, 0, k).wait_send()
                go_c(p, 1, k).wait_send()
                if k < NEAR_OUT or p == q:
                    share_y(p, k).wait_send()
            for h in range(2):
                for j in range(2):
                    for t in range(2):
                        share(plane(p), h, j, t).wait_send()
            if p != q:
                for at in range(2 * CHUNKS - NEAR_OUT):
                    share_z(AHEAD if p > q else BEHIND, q, p, at).wait_send()

    by_class(settle)


def scratch(n, rows, model, units, pad, hot):
    nz = n // 4
    half, full = jnp.bfloat16, jnp.float32
    dma = pltpu.SemaphoreType.DMA
    piece = rows // CHUNKS
    gathers, reduces = 2 * CHUNKS - NEAR_IN, 2 * CHUNKS - NEAR_OUT
    return [
        pltpu.VMEM((nz, 4, rows, model), half),
        pltpu.VMEM((nz, 2, rows, model), full),
        pltpu.VMEM((nz, 2, rows, model), half),
        pltpu.VMEM((nz, 2, rows, model), half),
        pltpu.VMEM((nz, rows, model), half),
        pltpu.VMEM((nz, rows, model), half),
        pltpu.VMEM((nz, reduces * piece, model), half),
        pltpu.VMEM((nz + 1, reduces * piece, model), half),
        pltpu.VMEM((model, units), half),
        pltpu.VMEM((model, units), half),
        pltpu.VMEM((units, model), half),
        pltpu.VMEM((3 * pad, model), half),
        pltpu.VMEM((2 * rows, units), half),
        pltpu.VMEM((2 * rows, pad), half),
        pltpu.VMEM((n, -(-(n + hot) // 8) * 8, rows), full),
        pltpu.VMEM((4, rows, 8), full),
        dma((3 + 3 * hot,)), dma, dma((nz,)), dma((nz,)), dma((nz,)),
        dma((nz,)), dma((nz,)), dma((nz, 2)), dma((nz, 2)),
        dma((nz, gathers)), dma((nz, gathers)), dma((nz, gathers)),
        dma((nz, CHUNKS)), dma((nz, CHUNKS)), dma((nz, 2, CHUNKS)), dma((nz, 2, CHUNKS)),
        dma((nz, 2, 2, 2)), dma((nz, 2, 2, 2)),
        dma((nz, CHUNKS)), dma((nz, CHUNKS)),
        dma((nz, reduces)), dma((nz + 1, reduces)),
    ]


def shards(tokens, w_gate, w_up, w_down, hot_gate, hot_up, hot_down, cold_routes, hot_pick, gates):
    n = lax.axis_size("expert")
    micro_count, local_tokens, model = tokens.shape
    rows = micro_count * local_tokens
    hot, units, part = hot_gate.shape[0], w_gate.shape[2], hot_gate.shape[2]
    pad = -(-hot * part // 128) * 128
    need = rows * model * n * 9 + 3 * model * (units + pad) * 2
    if n != 16 or part % 16 or rows % (16 * CHUNKS) or units % 384 or model % 256 or need > ROOM or hot > 7:
        return routed(
            tokens, w_gate, w_up, w_down, hot_gate, hot_up, hot_down, cold_routes, hot_pick, gates
        )
    anyplace = pl.BlockSpec(memory_space=pl.ANY)
    vmem = pl.BlockSpec(memory_space=pltpu.VMEM)
    mixed = pl.pallas_call(
        functools.partial(fused, n, hot, part),
        out_shape=jax.ShapeDtypeStruct((rows, model), jnp.bfloat16),
        in_specs=[anyplace, vmem, vmem, vmem] + [anyplace] * 6,
        out_specs=vmem,
        scratch_shapes=scratch(n, rows, model, units, pad, hot),
        compiler_params=pltpu.CompilerParams(
            collective_id=0, has_side_effects=True, vmem_limit_bytes=64 * 2**20 - 2**17
        ),
    )(
        tokens.reshape(rows, model), jnp.transpose(cold_routes, (2, 0, 1)), hot_pick,
        jnp.swapaxes(gates, 1, 2),
        w_gate[0], w_up[0], w_down[0],
        *(jnp.swapaxes(w, 1, 2) for w in (hot_gate, hot_up, hot_down)),
    )
    return mixed.reshape(tokens.shape)


def solution(mesh):
    in_specs = (
        P(None, ("groups", "expert"), None),
        P("expert", None, None),
        P("expert", None, None),
        P("expert", None, None),
        P(None, None, "expert"),
        P(None, None, "expert"),
        P(None, None, "expert"),
        P(None, ("groups", "expert"), None),
        P(None, ("groups", "expert")),
        P(None, ("groups", "expert"), None),
    )
    out_specs = P(None, ("groups", "expert"), None)
    return jax.shard_map(shards, mesh=mesh, in_specs=in_specs, out_specs=out_specs, check_vma=False)
```
